256 devices in a mesh: rows: 16 (over y, z_lo), cols: 16 (over x, z_hi, core).
Axes of the slice: x: 4, y: 4, z: 8 (z_hi: 2, z_lo: 4; z = z_hi * 4 + z_lo), core: 2. Of those that a mesh axis runs over, the one named last changes fastest.
Arguments:
- activations: bfloat16 [256, 256, 384], P('rows', 'cols'), may hold values from -6 to 6
- grad_out: bfloat16 [256, 256, 384], P('rows', 'cols'), may hold values from -6 to 6
- kernels: float32 [2, 7, 7, 384], replicated, may hold values from -0.875 to 0.875
- norm_gains: float32 [2, 384], replicated, may hold values from 0.5 to 1.5
- norm_shifts: float32 [2, 384], replicated, may hold values from -3 to 3
- w_in: bfloat16 [2, 384, 1536], replicated, may hold values from -0.3125 to 0.3125
- b_in: float32 [2, 1536], replicated, may hold values from -3 to 3
- w_out: bfloat16 [2, 384, 1536], replicated, may hold values from -0.15625 to 0.15625
Outputs:
- grad_in: bfloat16 [256, 256, 384], P('rows', 'cols')
- grad_kernels: float32 [2, 7, 7, 384], replicated
- grad_gains: float32 [2, 384], replicated
- grad_shifts: float32 [2, 384], replicated
- grad_b_in: float32 [2, 1536], replicated
- grad_w_in: float32 [2, 384, 1536], P(None, None, ('rows', 'cols'))
- grad_w_out: float32 [2, 384, 1536], P(None, None, ('rows', 'cols'))
The draws below stay inside these ranges and needn't reach their ends.
All inputs are finite; a program needn't handle non-finite values.
Results may differ from the reference program's by a relative error of at most 0.017.
Values may be sent and summed in bfloat16 or wider, within the bound.
A program may use at most 128 MiB of HBM per device.

```python
import math
import jax
import jax.numpy as jnp
from jax import lax

C = 384
HID = 1536
LAYERS = 2
NR = 256
NC = 256


def shard_levels(rng, dims, shards, smallest, top_value):
    def one(dim, shards_of):
        heights = jax.random.uniform(jax.random.fold_in(jax.random.fold_in(rng, 6), dim), (shards_of,), jnp.float32, smallest / len(shards), top_value / len(shards))
        return jnp.repeat(jnp.exp(heights), dims[dim] // shards_of).reshape((-1,) + (1,) * (len(dims) - dim - 1))

    factor_of = one(*shards[0])
    for cut in shards[1:]:
        factor_of = factor_of * one(*cut)
    return factor_of


def normal_values(rng, dims, scale, most, cuts=(), held_as=jnp.bfloat16):
    entries = jax.random.normal(rng, dims, jnp.float32) * scale
    if len(cuts) > 0:
        entries = shard_levels(rng, dims, cuts, -0.22, 0.18) * entries
    return jnp.clip(entries, min=-most, max=most).astype(held_as)


def setup_inputs(seed: int = 0) -> dict:
    key_of = jax.random.split(jax.random.key(seed), 9)
    return {
        "activations": normal_values(key_of[0], (NR, NC, C), 1.0, 6.0, ((0, 16), (1, 16))),
        "grad_out": normal_values(key_of[1], (NR, NC, C), 1.0, 6.0, ((0, 16), (1, 16))),
        "kernels": normal_values(key_of[2], (LAYERS, 7, 7, C), 49 ** -0.5, 0.875, (), jnp.float32),
        "norm_gains": jnp.clip(1.0 + 0.1 * jax.random.normal(key_of[3], (LAYERS, C), jnp.float32), 0.5, 1.5),
        "norm_shifts": normal_values(key_of[4], (LAYERS, C), 0.5, 3.0, (), jnp.float32),
        "w_in": normal_values(key_of[5], (LAYERS, C, HID), C ** -0.5, 0.3125),
        "b_in": normal_values(key_of[6], (LAYERS, HID), 0.5, 3.0, (), jnp.float32),
        "w_out": normal_values(key_of[7], (LAYERS, C, HID), HID ** -0.5, 0.15625),
    }


EPSILON = 1e-06
ROOT_HALF = 0.7071067811865476
INV_ROOT_TAU = 0.3989422804014327

def gelu_parts(pre_act):
    normal_cdf = 0.5 * (1.0 + lax.erf(pre_act * ROOT_HALF))
    density = jnp.exp(-0.5 * pre_act * pre_act) * INV_ROOT_TAU
    return (pre_act * normal_cdf, normal_cdf + pre_act * density)

def conv_from(padded, kernel, out_rows, out_cols):
    running = jnp.zeros((out_rows, out_cols, padded.shape[2]), jnp.float32)
    for row_off in range(7):
        for col_off in range(7):
            running = running + kernel[row_off, col_off] * padded[row_off:row_off + out_rows, col_off:col_off + out_cols]
    return running

def conv_back(padded_grad, kernel, out_rows, out_cols):
    running = jnp.zeros((out_rows, out_cols, padded_grad.shape[2]), jnp.float32)
    for row_off in range(7):
        for col_off in range(7):
            running = running + kernel[row_off, col_off] * padded_grad[6 - row_off:6 - row_off + out_rows, 6 - col_off:6 - col_off + out_cols]
    return running

def kernel_grad(grad_z, padded_in):
    out_rows, out_cols = (grad_z.shape[0], grad_z.shape[1])
    kernel_taps = []
    for row_off in range(7):
        for col_off in range(7):
            kernel_taps.append(lax.optimization_barrier(jnp.sum(grad_z * padded_in[row_off:row_off + out_rows, col_off:col_off + out_cols], axis=(0, 1))))
    return jnp.stack(kernel_taps).reshape(7, 7, grad_z.shape[2])

def norm_fwd(source, gain, shift):
    center = source - lax.optimization_barrier(jnp.mean(source, axis=-1, keepdims=True))
    inv_std = lax.rsqrt(lax.optimization_barrier(jnp.mean(center * center, axis=-1, keepdims=True)) + EPSILON)
    norm_hat = center * inv_std
    return (norm_hat, inv_std, (norm_hat * gain + shift).astype(jnp.bfloat16))

def norm_back(grad_n, norm_hat, inv_std, gain):
    scaled = grad_n * gain
    return inv_std * (scaled - lax.optimization_barrier(jnp.mean(scaled, axis=-1, keepdims=True)) - norm_hat * lax.optimization_barrier(jnp.mean(scaled * norm_hat, axis=-1, keepdims=True)))

def mlp_out(normed, weight_in, bias_in, weight_out, block_len):
    channels = normed.shape[1]

    def one_block(normed_block):
        pre_act = jnp.dot(normed_block, weight_in, preferred_element_type=jnp.float32) + bias_in
        act_b = gelu_parts(pre_act)[0].astype(jnp.bfloat16)
        return lax.dot_general(act_b, weight_out, (((1,), (1,)), ((), ())), preferred_element_type=jnp.float32)
    return lax.map(one_block, normed.reshape(-1, block_len, channels)).reshape(-1, channels)

def mlp_back(normed, grad_b, weight_in, bias_in, weight_out, block_len):
    channels = normed.shape[1]
    hidden = weight_in.shape[1]

    def one_block(running, block_pair):
        normed_block, grad_block = block_pair
        pre_act = jnp.dot(normed_block, weight_in, preferred_element_type=jnp.float32) + bias_in
        activation, gelu_slope = gelu_parts(pre_act)
        act_b = activation.astype(jnp.bfloat16)
        grad_wo = lax.dot_general(grad_block, act_b, (((0,), (0,)), ((), ())), preferred_element_type=jnp.float32)
        grad_pre = jnp.dot(grad_block, weight_out, preferred_element_type=jnp.float32) * gelu_slope
        grad_preb = grad_pre.astype(jnp.bfloat16)
        grad_wi = lax.dot_general(normed_block, grad_preb, (((0,), (0,)), ((), ())), preferred_element_type=jnp.float32)
        grad_n = lax.dot_general(grad_preb, weight_in, (((1,), (1,)), ((), ())), preferred_element_type=jnp.float32)
        return ((running[0] + grad_wi, running[1] + grad_wo, running[2] + lax.optimization_barrier(jnp.sum(grad_pre, axis=0))), grad_n)
    initial = (jnp.zeros((channels, hidden), jnp.float32), jnp.zeros((channels, hidden), jnp.float32), jnp.zeros((hidden,), jnp.float32))
    totals, grad_n = lax.scan(one_block, initial, (normed.reshape(-1, block_len, channels), grad_b.reshape(-1, block_len, channels)))
    return (totals, grad_n.reshape(-1, channels))

def layer_back(grad_b, normed, norm_hat, inv_std, padded_in, layer, kernels, norm_gains, w_in, b_in, w_out, block_len):
    image_rows, image_cols, channels = grad_b.shape
    totals, grad_n = mlp_back(normed.reshape(-1, channels), grad_b.reshape(-1, channels), w_in[layer], b_in[layer], w_out[layer], block_len)
    grad_n = grad_n.reshape(grad_b.shape)
    grad_gain = lax.optimization_barrier(jnp.sum(grad_n * norm_hat, axis=(0, 1)))
    grad_shift = lax.optimization_barrier(jnp.sum(grad_n, axis=(0, 1)))
    grad_z = norm_back(grad_n, norm_hat, inv_std, norm_gains[layer]).astype(jnp.bfloat16).astype(jnp.float32)
    kernel_taps = kernel_grad(grad_z, padded_in)
    spread = conv_back(jnp.pad(grad_z, ((3, 3), (3, 3), (0, 0))), kernels[layer], image_rows, image_cols)
    return (spread, kernel_taps, grad_gain, grad_shift, totals)

def reference(activations, grad_out, kernels, norm_gains, norm_shifts, w_in, b_in, w_out):
    image_rows, image_cols, channels = activations.shape
    pixels = image_rows * image_cols
    grad_scale = 1.0 / math.sqrt(pixels)
    block_len = math.gcd(pixels, 4096)
    inputs = activations.astype(jnp.float32)
    padded_in = jnp.pad(inputs, ((3, 3), (3, 3), (0, 0)))
    conv_one = conv_from(padded_in, kernels[0], image_rows, image_cols)
    hat_one, inv_one, normed_one = norm_fwd(conv_one, norm_gains[0], norm_shifts[0])
    mixed_one = mlp_out(normed_one.reshape(-1, channels), w_in[0], b_in[0], w_out[0], block_len)
    middle = (inputs + mixed_one.reshape(inputs.shape)).astype(jnp.bfloat16)
    padded_mid = jnp.pad(middle.astype(jnp.float32), ((3, 3), (3, 3), (0, 0)))
    conv_two = conv_from(padded_mid, kernels[1], image_rows, image_cols)
    hat_two, inv_two, normed_two = norm_fwd(conv_two, norm_gains[1], norm_shifts[1])
    back_two = layer_back(grad_out, normed_two, hat_two, inv_two, padded_mid, 1, kernels, norm_gains, w_in, b_in, w_out, block_len)
    grad_mid = (grad_out.astype(jnp.float32) + back_two[0]).astype(jnp.bfloat16)
    back_one = layer_back(grad_mid, normed_one, hat_one, inv_one, padded_in, 0, kernels, norm_gains, w_in, b_in, w_out, block_len)
    grad_in = (grad_mid.astype(jnp.float32) + back_one[0]).astype(jnp.bfloat16)
    grad_kernels = jnp.stack([back_one[1], back_two[1]]) * grad_scale
    grad_gains = jnp.stack([back_one[2], back_two[2]]) * grad_scale
    grad_shifts = jnp.stack([back_one[3], back_two[3]]) * grad_scale
    grad_b_in = jnp.stack([back_one[4][2], back_two[4][2]]) * grad_scale
    grad_w_in = jnp.stack([back_one[4][0], back_two[4][0]]) * grad_scale
    grad_w_out = jnp.stack([back_one[4][1], back_two[4][1]]) * grad_scale
    return (grad_in, grad_kernels, grad_gains, grad_shifts, grad_b_in, grad_w_in, grad_w_out)
```

```python
import functools
import math

import jax
import jax.numpy as jnp
from jax import lax
from jax.experimental import pallas as pl
from jax.experimental.pallas import tpu as pltpu
from jax.sharding import PartitionSpec as P

EPSILON = 1e-06
ROOT_HALF = 0.7071067811865476
INV_ROOT_TAU = 0.3989422804014327
MESH = pl.DeviceIdType.MESH
F32 = jnp.float32
BF16 = jnp.bfloat16

C = 384
HID = 1536
TILE = 16
PIX = TILE * TILE
PITCH = 32
PROWS = TILE + 6
GROUPS = C // 128
CHUNK = 256
SMALL = 64
DIRS = tuple((dr, dc) for dr in (-1, 0, 1) for dc in (-1, 0, 1) if (dr, dc) != (0, 0))
TN = (((0,), (0,)), ((), ()))
NT = (((1,), (1,)), ((), ()))


def lanes(g):
    return pl.ds(g * 128, 128)


def gelu_parts(pre):
    cdf = 0.5 * (1.0 + lax.erf(pre * ROOT_HALF))
    density = jnp.exp(-0.5 * pre * pre) * INV_ROOT_TAU
    return pre * cdf, cdf + pre * density


def pad_row(i):
    return (i + 3) * PITCH + 8


def conv_into(src, kern, layer, flip, emit):
    block = 4

    def step(it, carry):
        g = it // (TILE // block)
        row = (it % (TILE // block)) * block
        col = pl.ds(pl.multiple_of(g * 128, 128), 128)
        acc = [[None, None] for _ in range(block)]
        for rho in range(block + 6):
            taps = [
                src[g, pl.ds((row + rho) * PITCH + 5 + s, 8, stride=2), :] for s in range(8)
            ]
            for i in range(block):
                a = rho - i
                if a < 0 or a > 6:
                    continue
                for b in range(7):
                    ka, kb = (6 - a, 6 - b) if flip else (a, b)
                    w = kern[layer, ka, pl.ds(kb, 1), col]
                    for par in range(2):
                        term = taps[b + par] * w
                        acc[i][par] = term if acc[i][par] is None else acc[i][par] + term
        for i in range(block):
            for par in range(2):
                emit(g, row + i, par, acc[i][par])
        return carry

    lax.fori_loop(0, GROUPS * (TILE // block), step, 0)


def taps_grad(grad, src, small, layer):
    def step(it, carry):
        g = it // 7
        a = it % 7
        col = pl.ds(pl.multiple_of(g * 128, 128), 128)
        acc = [None] * 7
        for i in range(TILE):
            dz = [grad[g, pl.ds(pad_row(i) + par, 8, stride=2), :] for par in range(2)]
            row = [src[g, pl.ds((i + a) * PITCH + 5 + s, 8, stride=2), :] for s in range(8)]
            for b in range(7):
                term = dz[0] * row[b] + dz[1] * row[b + 1]
                acc[b] = term if acc[b] is None else acc[b] + term
        rows = [jnp.sum(acc[b], axis=0, keepdims=True) for b in range(7)]
        rows.append(jnp.zeros((1, 128), F32))
        small[layer, pl.ds(pl.multiple_of(a * 8, 8), 8), col] = jnp.concatenate(rows, axis=0)
        return carry

    lax.fori_loop(0, GROUPS * 7, step, 0)


def kernel(
    act_ref,
    gout_ref,
    kern_ref,
    gain_ref,
    shift_ref,
    win_hbm,
    bin_ref,
    wout_hbm,
    gin_ref,
    gk_ref,
    gg_ref,
    gs_ref,
    gb_ref,
    gwi_ref,
    gwo_ref,
    win,
    wout,
    pads,
    z_ref,
    hat_ref,
    inv_ref,
    hid_ref,
    gn_ref,
    slope_ref,
    ga_ref,
    pre_ref,
    dn_ref,
    db_ref,
    red_ref,
    hsend,
    hrecv,
    csend,
    crecv,
    s1,
    r1,
    own1,
    s2,
    r2,
    own2,
    s3,
    r3,
    fsend,
    frecv,
    small,
    smc,
    smt,
    sma,
    smb,
    smz,
    smg,
    smx,
    wsem,
    hs,
    hr,
    cs,
    cr,
    p1s,
    p1r,
    p2s,
    p2r,
    p3s,
    p3r,
    fs,
    fr,
    mcs,
    mcr,
    mas,
    mar,
    mbs,
    mbr,
    mzs,
    mzr,
    mgs,
    mgr,
    mxs,
    mxr,
):
    r = lax.axis_index("rows")
    c = lax.axis_index("cols")
    y, zl = r // 4, r % 4
    x, zh, core = c // 4, (c // 2) % 2, c % 2
    z = zh * 4 + zl
    first = y * (1 - core) + x * core
    second = x * (1 - core) + y * core
    scale = 1.0 / math.sqrt(256 * 256)

    def device(dx, dy, dz, dcore):
        return (dy * 4 + dz % 4, dx * 4 + (dz // 4) * 2 + dcore)

    def first_peer(k):
        q = (first + k) % 4
        return device(x * (1 - core) + q * core, q * (1 - core) + y * core, z, core)

    def second_peer(k):
        q = (second + k) % 4
        return device(q * (1 - core) + x * core, y * (1 - core) + q * core, z, core)

    def z_peer(k):
        return device(x, y, (z + k) % 8, core)

    def last_target(q):
        return device(q // 2, first, (q % 2) * 4 + second, core)

    def last_source(zs):
        return device(zl * (1 - core) + y * core, y * (1 - core) + zl * core, zs, core)

    partner = (r, c + 1 - 2 * core)

    def is_me(dev):
        return jnp.logical_and(dev[0] == r, dev[1] == c)

    def exists(d):
        rr, cc = r + d[0], c + d[1]
        return jnp.logical_and(
            jnp.logical_and(rr >= 0, rr < 16), jnp.logical_and(cc >= 0, cc < 16)
        )

    barrier = pltpu.get_barrier_semaphore()

    def greet(dev):
        pl.semaphore_signal(barrier, inc=1, device_id=dev, device_id_type=MESH)

    count = jnp.int32(13)
    for d in DIRS:
        ok = exists(d)

        @pl.when(ok)
        def _(d=d):
            greet((r + d[0], c + d[1]))

        count = count + ok.astype(jnp.int32)
    for k in range(1, 4):
        greet(first_peer(k))
        greet(second_peer(k))
    for k in range(1, 8):
        greet(z_peer(k))
    for q in range(8):
        for dev in (last_target(q), last_source(q)):
            away = jnp.logical_not(is_me(dev))

            @pl.when(away)
            def _(dev=dev):
                greet(dev)

            count = count + away.astype(jnp.int32)

    weight_copies = []
    for n, (src, dst, l) in enumerate(
        ((win_hbm, win, 0), (wout_hbm, wout, 0), (win_hbm, win, 1), (wout_hbm, wout, 1))
    ):
        copy = pltpu.make_async_copy(src.at[l], dst.at[l], wsem.at[n])
        copy.start()
        weight_copies.append(copy)

    zero = jnp.zeros((PITCH, 128), F32)

    def clear(it, carry):
        for p in range(4):
            for g in range(GROUPS):
                pads[p, g, pl.ds(pl.multiple_of(it * PITCH, PITCH), PITCH), :] = zero
        return carry

    lax.fori_loop(0, PROWS, clear, 0)

    def fill(it, carry):
        rows = pl.ds(pl.multiple_of(it * TILE, TILE), TILE)
        for g in range(GROUPS):
            pads[0, g, pl.ds(pl.multiple_of(pad_row(it), 8), TILE), :] = act_ref[
                rows, lanes(g)
            ].astype(F32)
        gn_ref[1, 1, rows, :] = gout_ref[rows, :]
        return carry

    lax.fori_loop(0, TILE, fill, 0)

    def halo_copy(e, n):
        d = DIRS[n]
        size = 32 if d[0] != 0 and d[1] != 0 else 48
        return pltpu.make_async_remote_copy(
            src_ref=hsend.at[e, n, pl.ds(0, size)],
            dst_ref=hrecv.at[e, 7 - n, pl.ds(0, size)],
            send_sem=hs.at[e, n],
            recv_sem=hr.at[e, 7 - n],
            device_id=(r + d[0], c + d[1]),
            device_id_type=MESH,
        )

    def halo_start(e, p):
        for n, d in enumerate(DIRS):
            row0 = {-1: 0, 0: 0, 1: TILE - 3}[d[0]]
            for g in range(GROUPS):
                if d[1] == 0:
                    for k in range(3):
                        hsend[e, n, pl.ds(k * 16, 16), lanes(g)] = pads[
                            p, g, pl.ds(pad_row(row0 + k), TILE), :
                        ].astype(BF16)
                elif d[0] == 0:
                    col0 = 0 if d[1] < 0 else TILE - 3
                    for k in range(3):
                        hsend[e, n, pl.ds(k * 16, 16), lanes(g)] = pads[
                            p, g, pl.ds(pad_row(0) + col0 + k, TILE, stride=PITCH), :
                        ].astype(BF16)
                else:
                    col0 = 0 if d[1] < 0 else 8
                    parts = [
                        pads[p, g, pl.ds(pad_row(row0 + k) + col0, 8), :] for k in range(3)
                    ]
                    hsend[e, n, pl.ds(0, 32), lanes(g)] = jnp.concatenate(
                        parts + [parts[2]], axis=0
                    ).astype(BF16)

            @pl.when(exists(d))
            def _(n=n):
                halo_copy(e, n).start()

    def halo_finish(e, p):
        for n, d in enumerate(DIRS):

            @pl.when(exists(d))
            def _(n=n, d=d):
                copy = halo_copy(e, n)
                copy.wait_send()
                size = 32 if d[0] != 0 and d[1] != 0 else 48
                pltpu.make_async_remote_copy(
                    src_ref=hsend.at[e, n, pl.ds(0, size)],
                    dst_ref=hrecv.at[e, n, pl.ds(0, size)],
                    send_sem=hs.at[e, n],
                    recv_sem=hr.at[e, n],
                    device_id=(r + d[0], c + d[1]),
                    device_id_type=MESH,
                ).wait_recv()
                row0 = {-1: -3, 0: 0, 1: TILE}[d[0]]
                for g in range(GROUPS):
                    got = hrecv[e, n, pl.ds(0, size), lanes(g)].astype(F32)
                    if d[1] == 0:
                        for k in range(3):
                            pads[p, g, pl.ds(pad_row(row0 + k), TILE), :] = got[
                                k * 16 : k * 16 + 16
                            ]
                    elif d[0] == 0:
                        col0 = -3 if d[1] < 0 else TILE
                        for k in range(3):
                            pads[
                                p, g, pl.ds(pad_row(0) + col0 + k, TILE, stride=PITCH), :
                            ] = got[k * 16 : k * 16 + 16]
                    else:
                        col0 = -8 if d[1] < 0 else TILE
                        for k in range(3):
                            pads[p, g, pl.ds(pad_row(row0 + k) + col0, 8), :] = got[
                                k * 8 : k * 8 + 8
                            ]

    pl.semaphore_wait(barrier, count)
    halo_start(0, 0)

    def forward_norm(layer, p):
        def emit(g, i, par, value):
            z_ref[g, pl.ds(i * TILE + par, 8, stride=2), :] = value

        conv_into(pads.at[p], kern_ref, layer, False, emit)

        def step(it, carry):
            rows = pl.ds(pl.multiple_of(it * 32, 32), 32)
            zs = [z_ref[g, rows, :] for g in range(GROUPS)]
            mean = jnp.sum(zs[0] + zs[1] + zs[2], axis=-1, keepdims=True) * (1.0 / C)
            cen = [v - mean for v in zs]
            var = jnp.sum(
                cen[0] * cen[0] + cen[1] * cen[1] + cen[2] * cen[2], axis=-1, keepdims=True
            ) * (1.0 / C)
            inv = lax.rsqrt(var + EPSILON)
            inv_ref[layer, rows, :] = jnp.broadcast_to(inv, (32, 128))
            for g in range(GROUPS):
                hat = cen[g] * inv
                hat_ref[layer, g, rows, :] = hat
                gn_ref[layer, 0, rows, lanes(g)] = (
                    hat * gain_ref[pl.ds(layer, 1), lanes(g)]
                    + shift_ref[pl.ds(layer, 1), lanes(g)]
                ).astype(BF16)
            return carry

        lax.fori_loop(0, PIX // 32, step, 0)

    def hidden_forward(layer):
        def step(n, carry):
            cols = pl.ds(pl.multiple_of(n * CHUNK, CHUNK), CHUNK)
            pre_ref[...] = jnp.dot(
                gn_ref[layer, 0], win[layer, :, cols], preferred_element_type=F32
            )
            bias = bin_ref[pl.ds(layer, 1), cols]

            def inner(it, carry):
                rows = pl.ds(pl.multiple_of(it * 32, 32), 32)
                act, slope = gelu_parts(pre_ref[rows, :] + bias)
                hid_ref[layer, 1, rows, cols] = act.astype(BF16)
                slope_ref[layer, rows, cols] = slope
                return carry

            lax.fori_loop(0, PIX // 32, inner, 0)
            return carry

        lax.fori_loop(0, HID // CHUNK, step, 0)

    def hidden_grad(layer):
        def step(n, carry):
            cols = pl.ds(pl.multiple_of(n * CHUNK, CHUNK), CHUNK)
            ga_ref[:, cols] = jnp.dot(
                gn_ref[layer, 1], wout[layer, :, cols], preferred_element_type=F32
            )
            return carry

        lax.fori_loop(0, HID // CHUNK, step, 0)

    def slope_times(layer):
        def step(n, carry):
            cols = pl.ds(pl.multiple_of(n * CHUNK, CHUNK), CHUNK)

            def inner(it, total):
                rows = pl.ds(pl.multiple_of(it * 32, 32), 32)
                grad = ga_ref[rows, cols] * slope_ref[layer, rows, cols]
                hid_ref[layer, 0, rows, cols] = grad.astype(BF16)
                return total + (grad[0:8] + grad[8:16]) + (grad[16:24] + grad[24:32])

            total = lax.fori_loop(0, PIX // 32, inner, jnp.zeros((8, CHUNK), F32))
            db_ref[pl.ds(layer, 1), cols] = jnp.sum(total, axis=0, keepdims=True)
            return carry

        lax.fori_loop(0, HID // CHUNK, step, 0)

    def norm_grad(layer, p):
        dn_ref[...] = lax.dot_general(
            hid_ref[layer, 0], win[layer], NT, preferred_element_type=F32
        )
        red_ref[...] = jnp.zeros_like(red_ref)

        def step(it, carry):
            rows = pl.ds(pl.multiple_of(it * 32, 32), 32)
            dn = [dn_ref[rows, lanes(g)] for g in range(GROUPS)]
            hat = [hat_ref[layer, g, rows, :] for g in range(GROUPS)]
            sc = [dn[g] * gain_ref[pl.ds(layer, 1), lanes(g)] for g in range(GROUPS)]
            m1 = jnp.sum(sc[0] + sc[1] + sc[2], axis=-1, keepdims=True) * (1.0 / C)
            m2 = jnp.sum(
                sc[0] * hat[0] + sc[1] * hat[1] + sc[2] * hat[2], axis=-1, keepdims=True
            ) * (1.0 / C)
            inv = inv_ref[layer, rows, :]
            for g in range(GROUPS):
                dz = (inv * (sc[g] - m1 - hat[g] * m2)).astype(BF16).astype(F32)
                for k in range(2):
                    pads[
                        p, g, pl.ds(pl.multiple_of(pad_row(it * 2 + k), 8), TILE), :
                    ] = dz[k * TILE : (k + 1) * TILE]
                prod = dn[g] * hat[g]
                red_ref[0, :, lanes(g)] += (prod[0:8] + prod[8:16]) + (prod[16:24] + prod[24:32])
                red_ref[1, :, lanes(g)] += (dn[g][0:8] + dn[g][8:16]) + (
                    dn[g][16:24] + dn[g][24:32]
                )
            return carry

        lax.fori_loop(0, PIX // 32, step, 0)
        small[layer, pl.ds(56, 1), :] = jnp.sum(red_ref[0], axis=0, keepdims=True)
        small[layer, pl.ds(57, 1), :] = jnp.sum(red_ref[1], axis=0, keepdims=True)
        for k in range(4):
            small[layer, pl.ds(58 + k, 1), :] = db_ref[pl.ds(layer, 1), pl.ds(k * C, C)]
        small[layer, pl.ds(62, 2), :] = jnp.zeros((2, C), F32)

    def remote(src, dst, ssem, rsem, dev):
        return pltpu.make_async_remote_copy(
            src_ref=src,
            dst_ref=dst,
            send_sem=ssem,
            recv_sem=rsem,
            device_id=dev,
            device_id_type=MESH,
        )

    def pair_copy(l, q):
        return remote(csend.at[l, q], crecv.at[l, q], cs.at[l, q], cr.at[l, q], partner)

    def first_copy(l, k):
        return remote(
            s1.at[l, k - 1], r1.at[l, k - 1], p1s.at[l, k - 1], p1r.at[l, k - 1], first_peer(k)
        )

    def second_copy(l, k):
        return remote(
            s2.at[l, k - 1], r2.at[l, k - 1], p2s.at[l, k - 1], p2r.at[l, k - 1], second_peer(k)
        )

    def last_copy(l, q):
        return remote(s3.at[l, q], r3.at[l, z], p3s.at[l, q], p3r.at[l, z], last_target(q))

    def back_copy(l):
        return remote(fsend.at[l], frecv.at[l], fs.at[l], fr.at[l], partner)

    def weight_grad(l, m, q):
        return lax.dot_general(
            hid_ref[l, m, :, pl.ds(pl.multiple_of(q * C, C), C)],
            gn_ref[l, m],
            TN,
            preferred_element_type=F32,
        )

    def reduce_start(l):
        def away(q, carry):
            csend[l, q] = weight_grad(l, 1 - core, q).astype(BF16)
            pair_copy(l, q).start()
            return carry

        lax.fori_loop(0, 4, away, 0)

    def reduce_first(l):
        def block(k):
            q = (first + k) % 4
            mine = weight_grad(l, core, q)
            pair_copy(l, q).wait()
            return mine + crecv[l, q].astype(F32)

        def step(k, carry):
            s1[l, k - 1] = block(k).astype(BF16)
            first_copy(l, k).start()
            return carry

        lax.fori_loop(1, 4, step, 0)
        own1[...] = block(0)

    def reduce_second(l):
        for k in range(1, 4):
            first_copy(l, k).wait()

        def block(k):
            rows = pl.ds(pl.multiple_of(((second + k) % 4) * 96, 96), 96)
            return (
                own1[rows, :]
                + r1[l, 0, rows, :].astype(F32)
                + r1[l, 1, rows, :].astype(F32)
                + r1[l, 2, rows, :].astype(F32)
            )

        def step(k, carry):
            s2[l, k - 1] = block(k).astype(BF16)
            second_copy(l, k).start()
            return carry

        lax.fori_loop(1, 4, step, 0)
        own2[...] = block(0)

    def reduce_last(l):
        for k in range(1, 4):
            second_copy(l, k).wait()
        total = (
            own2[...]
            + r2[l, 0].astype(F32)
            + r2[l, 1].astype(F32)
            + r2[l, 2].astype(F32)
        )
        pad = jnp.zeros((4, C), F32)
        for q in range(8):
            s3[l, q] = jnp.concatenate([total[12 * q : 12 * q + 12], pad], axis=0).astype(BF16)
            me = is_me(last_target(q))

            @pl.when(jnp.logical_not(me))
            def _(q=q):
                last_copy(l, q).start()

            @pl.when(me)
            def _(q=q):
                r3[l, z] = s3[l, q]

    def reduce_back(l):
        for q in range(8):

            @pl.when(jnp.logical_not(is_me(last_target(q))))
            def _(q=q):
                last_copy(l, q).wait_send()

            @pl.when(jnp.logical_not(is_me(last_source(q))))
            def _(q=q):
                remote(
                    s3.at[l, 0], r3.at[l, q], p3s.at[l, 0], p3r.at[l, q], last_source(q)
                ).wait_recv()

        total = r3[l, 0].astype(F32)
        for q in range(1, 8):
            total = total + r3[l, q].astype(F32)
        total = total * scale
        pad = jnp.zeros((2, C), F32)
        low = jnp.concatenate([total[0:6], pad], axis=0)
        high = jnp.concatenate([total[6:12], pad], axis=0)
        zeroth = core == 0
        fsend[l] = jnp.where(zeroth, high, low)
        back_copy(l).start()
        return jnp.where(zeroth, low, high)

    def reduce_end(l, mine):
        back_copy(l).wait()
        other = frecv[l]
        zeroth = core == 0
        gwi_ref[l] = jnp.where(zeroth, mine, other)
        gwo_ref[l] = jnp.where(zeroth, other, mine)

    def small_pair(l):
        half = pl.ds(pl.multiple_of((1 - core) * 32, 32), 32)
        return remote(small.at[l, half], smc.at[l], mcs.at[l], mcr.at[l], partner)

    def small_first(l, k):
        q = (first + k) % 4
        return remote(
            smt.at[l, q], sma.at[l, k - 1], mas.at[l, k - 1], mar.at[l, k - 1], first_peer(k)
        )

    def small_second(l, k):
        return remote(
            smb.at[l, second],
            smb.at[l, second],
            mbs.at[l, k - 1],
            mbr.at[l, k - 1],
            second_peer(k),
        )

    def small_z(l, k):
        return remote(
            smz.at[l, z], smz.at[l, z], mzs.at[l, k - 1], mzr.at[l, k - 1], z_peer(k)
        )

    def small_gather(l, k):
        return remote(
            smg.at[l, first], smg.at[l, first], mgs.at[l, k - 1], mgr.at[l, k - 1], first_peer(k)
        )

    def small_back(l):
        return remote(smg.at[l], smx.at[l], mxs.at[l], mxr.at[l], partner)

    def small_0(l):
        small_pair(l).start()

    def small_1(l):
        small_pair(l).wait()
        for q in range(4):
            rows = pl.ds(pl.multiple_of(core * 32 + q * 8, 8), 8)
            smt[l, q] = small[l, rows, :] + smc[l, pl.ds(q * 8, 8), :]
        for k in range(1, 4):
            small_first(l, k).start()

    def small_2(l):
        for k in range(1, 4):
            small_first(l, k).wait()
        smb[l, second] = (smt[l, first] + sma[l, 0]) + (sma[l, 1] + sma[l, 2])
        for k in range(1, 4):
            small_second(l, k).start()

    def small_3(l):
        for k in range(1, 4):
            small_second(l, k).wait()
        smz[l, z] = (smb[l, 0] + smb[l, 1]) + (smb[l, 2] + smb[l, 3])
        for k in range(1, 8):
            small_z(l, k).start()

    def small_4(l):
        for k in range(1, 8):
            small_z(l, k).wait()
        total = smz[l, 0]
        for q in range(1, 8):
            total = total + smz[l, q]
        smg[l, first] = total * scale
        for k in range(1, 4):
            small_gather(l, k).start()

    def small_5(l):
        for k in range(1, 4):
            small_gather(l, k).wait()
        small_back(l).start()

    def small_6(l):
        small_back(l).wait()
        zeroth = core == 0
        low = [jnp.where(zeroth, smg[l, q], smx[l, q]) for q in range(4)]
        high = [jnp.where(zeroth, smx[l, q], smg[l, q]) for q in range(4)]
        full = jnp.concatenate(low + high, axis=0)
        for a in range(7):
            gk_ref[l, a] = full[a * 8 : a * 8 + 7]
        gg_ref[pl.ds(l, 1), :] = full[56:57]
        gs_ref[pl.ds(l, 1), :] = full[57:58]
        for k in range(4):
            gb_ref[pl.ds(l, 1), pl.ds(k * C, C)] = full[58 + k : 59 + k]

    for copy in weight_copies:
        copy.wait()
    hidden_grad(1)
    halo_finish(0, 0)
    forward_norm(0, 0)
    hidden_forward(0)
    dn_ref[...] = lax.dot_general(hid_ref[0, 1], wout[0], NT, preferred_element_type=F32)

    def to_middle(it, carry):
        rows = pl.ds(pl.multiple_of(it * TILE, TILE), TILE)
        at = pl.ds(pl.multiple_of(pad_row(it), 8), TILE)
        for g in range(GROUPS):
            pads[1, g, at, :] = (pads[0, g, at, :] + dn_ref[rows, lanes(g)]).astype(BF16).astype(F32)
        return carry

    lax.fori_loop(0, TILE, to_middle, 0)
    halo_start(1, 1)
    halo_finish(1, 1)
    forward_norm(1, 1)
    hidden_forward(1)
    slope_times(1)
    norm_grad(1, 2)
    halo_start(2, 2)
    reduce_start(1)
    taps_grad(pads.at[2], pads.at[1], small, 1)
    small_0(1)
    reduce_first(1)
    halo_finish(2, 2)

    def emit_mid(g, i, par, value):
        z_ref[g, pl.ds(i * TILE + par, 8, stride=2), :] = value

    conv_into(pads.at[2], kern_ref, 1, True, emit_mid)

    def to_grad_mid(it, carry):
        rows = pl.ds(pl.multiple_of(it * 32, 32), 32)
        for g in range(GROUPS):
            gn_ref[0, 1, rows, lanes(g)] = (
                gn_ref[1, 1, rows, lanes(g)].astype(F32) + z_ref[g, rows, :]
            ).astype(BF16)
        return carry

    lax.fori_loop(0, PIX // 32, to_grad_mid, 0)
    small_1(1)
    hidden_grad(0)
    slope_times(0)
    reduce_second(1)
    small_2(1)
    norm_grad(0, 3)
    halo_start(3, 3)
    reduce_start(0)
    reduce_last(1)
    small_3(1)
    reduce_first(0)
    mine_1 = reduce_back(1)
    small_4(1)
    taps_grad(pads.at[3], pads.at[0], small, 0)
    small_0(0)
    small_5(1)
    halo_finish(3, 3)
    small_1(0)
    conv_into(pads.at[3], kern_ref, 0, True, emit_mid)

    def to_grad_in(it, carry):
        rows = pl.ds(pl.multiple_of(it * 32, 32), 32)
        for g in range(GROUPS):
            gin_ref[rows, lanes(g)] = (
                gn_ref[0, 1, rows, lanes(g)].astype(F32) + z_ref[g, rows, :]
            ).astype(BF16)
        return carry

    lax.fori_loop(0, PIX // 32, to_grad_in, 0)
    reduce_end(1, mine_1)
    small_6(1)
    small_2(0)
    small_3(0)
    reduce_second(0)
    small_4(0)
    reduce_last(0)
    small_5(0)
    mine_0 = reduce_back(0)
    small_6(0)
    reduce_end(0, mine_0)


def shards(activations, grad_out, kernels, norm_gains, norm_shifts, w_in, b_in, w_out):
    vmem = pl.BlockSpec(memory_space=pltpu.VMEM)
    hbm = pl.BlockSpec(memory_space=pl.ANY)
    dma = pltpu.SemaphoreType.DMA
    pad_size = PROWS * PITCH
    scratch = [
        pltpu.VMEM((2, C, HID), BF16),
        pltpu.VMEM((2, C, HID), BF16),
        pltpu.VMEM((4, GROUPS, pad_size, 128), F32),
        pltpu.VMEM((GROUPS, PIX, 128), F32),
        pltpu.VMEM((2, GROUPS, PIX, 128), F32),
        pltpu.VMEM((2, PIX, 128), F32),
        pltpu.VMEM((2, 2, PIX, HID), BF16),
        pltpu.VMEM((2, 2, PIX, C), BF16),
        pltpu.VMEM((2, PIX, HID), F32),
        pltpu.VMEM((PIX, HID), F32),
        pltpu.VMEM((PIX, CHUNK), F32),
        pltpu.VMEM((PIX, C), F32),
        pltpu.VMEM((2, HID), F32),
        pltpu.VMEM((2, 8, C), F32),
        pltpu.VMEM((4, 8, 48, C), BF16),
        pltpu.VMEM((4, 8, 48, C), BF16),
        pltpu.VMEM((2, 4, C, C), BF16),
        pltpu.VMEM((2, 4, C, C), BF16),
        pltpu.VMEM((2, 3, C, C), BF16),
        pltpu.VMEM((2, 3, C, C), BF16),
        pltpu.VMEM((C, C), F32),
        pltpu.VMEM((2, 3, 96, C), BF16),
        pltpu.VMEM((2, 3, 96, C), BF16),
        pltpu.VMEM((96, C), F32),
        pltpu.VMEM((2, 8, 16, C), BF16),
        pltpu.VMEM((2, 8, 16, C), BF16),
        pltpu.VMEM((2, 8, C), F32),
        pltpu.VMEM((2, 8, C), F32),
        pltpu.VMEM((2, SMALL, C), F32),
        pltpu.VMEM((2, 32, C), F32),
        pltpu.VMEM((2, 4, 8, C), F32),
        pltpu.VMEM((2, 3, 8, C), F32),
        pltpu.VMEM((2, 4, 8, C), F32),
        pltpu.VMEM((2, 8, 8, C), F32),
        pltpu.VMEM((2, 4, 8, C), F32),
        pltpu.VMEM((2, 4, 8, C), F32),
        dma((4,)),
        dma((4, 8)),
        dma((4, 8)),
        dma((2, 4)),
        dma((2, 4)),
        dma((2, 3)),
        dma((2, 3)),
        dma((2, 3)),
        dma((2, 3)),
        dma((2, 8)),
        dma((2, 8)),
        dma((2,)),
        dma((2,)),
        dma((2,)),
        dma((2,)),
        dma((2, 3)),
        dma((2, 3)),
        dma((2, 3)),
        dma((2, 3)),
        dma((2, 7)),
        dma((2, 7)),
        dma((2, 3)),
        dma((2, 3)),
        dma((2,)),
        dma((2,)),
    ]
    sds = jax.ShapeDtypeStruct
    outs = pl.pallas_call(
        kernel,
        out_shape=(
            sds((PIX, C), BF16),
            sds((2, 7, 7, C), F32),
            sds((2, C), F32),
            sds((2, C), F32),
            sds((2, HID), F32),
            sds((2, 8, C), F32),
            sds((2, 8, C), F32),
        ),
        in_specs=[vmem, vmem, vmem, vmem, vmem, hbm, vmem, hbm],
        out_specs=(vmem,) * 7,
        scratch_shapes=scratch,
        compiler_params=pltpu.CompilerParams(
            collective_id=0, has_side_effects=True, vmem_limit_bytes=64000000
        ),
        name="convnext_step",
    )(
        activations.reshape(PIX, C),
        grad_out.reshape(PIX, C),
        kernels,
        norm_gains,
        norm_shifts,
        w_in,
        b_in,
        w_out,
    )
    grad_in, gk, gg, gs, gb, gwi, gwo = outs
    return (
        grad_in.reshape(activations.shape),
        gk,
        gg,
        gs,
        gb,
        jnp.swapaxes(gwi[:, :6], 1, 2),
        jnp.swapaxes(gwo[:, :6], 1, 2),
    )


def solution(mesh):
    return jax.shard_map(
        shards,
        mesh=mesh,
        in_specs=(P("rows", "cols", None), P("rows", "cols", None), P(), P(), P(), P(), P(), P()),
        out_specs=(
            P("rows", "cols", None),
            P(),
            P(),
            P(),
            P(),
            P(None, None, ("rows", "cols")),
            P(None, None, ("rows", "cols")),
        ),
        check_vma=False,
    )
```

```python
import functools
import math

import jax
import jax.numpy as jnp
from jax import lax
from jax.experimental import pallas as pl
from jax.experimental.pallas import tpu as pltpu
from jax.sharding import PartitionSpec as P

EPSILON = 1e-06
ROOT_HALF = 0.7071067811865476
INV_ROOT_TAU = 0.3989422804014327
MESH = pl.DeviceIdType.MESH
F32 = jnp.float32
BF16 = jnp.bfloat16

C = 384
HID = 1536
TILE = 16
PIX = TILE * TILE
PITCH = 32
PROWS = TILE + 6
GROUPS = C // 128
CHUNK = 256
SMALL = 64
DIRS = tuple((dr, dc) for dr in (-1, 0, 1) for dc in (-1, 0, 1) if (dr, dc) != (0, 0))
TN = (((0,), (0,)), ((), ()))
NT = (((1,), (1,)), ((), ()))


def lanes(g):
    return pl.ds(g * 128, 128)


def gelu_parts(pre):
    cdf = 0.5 * (1.0 + lax.erf(pre * ROOT_HALF))
    density = jnp.exp(-0.5 * pre * pre) * INV_ROOT_TAU
    return pre * cdf, cdf + pre * density


def pad_row(i):
    return (i + 3) * PITCH + 8


def conv_into(src, kern, layer, flip, emit):
    block = 4

    def step(it, carry):
        g = it // (TILE // block)
        row = (it % (TILE // block)) * block
        col = pl.ds(pl.multiple_of(g * 128, 128), 128)
        acc = [[None, None] for _ in range(block)]
        for rho in range(block + 6):
            taps = [
                src[g, pl.ds((row + rho) * PITCH + 5 + s, 8, stride=2), :] for s in range(8)
            ]
            for i in range(block):
                a = rho - i
                if a < 0 or a > 6:
                    continue
                for b in range(7):
                    ka, kb = (6 - a, 6 - b) if flip else (a, b)
                    w = kern[ka, kb, pl.ds(layer, 1), col]
                    for par in range(2):
                        term = taps[b + par] * w
                        acc[i][par] = term if acc[i][par] is None else acc[i][par] + term
        for i in range(block):
            for par in range(2):
                emit(g, row + i, par, acc[i][par])
        return carry

    lax.fori_loop(0, GROUPS * (TILE // block), step, 0)


def taps_grad(grad, src, small, layer):
    def step(it, carry):
        g = it // 7
        a = it % 7
        col = pl.ds(pl.multiple_of(g * 128, 128), 128)
        acc = [None] * 7
        for i in range(TILE):
            dz = [grad[g, pl.ds(pad_row(i) + par, 8, stride=2), :] for par in range(2)]
            row = [src[g, pl.ds((i + a) * PITCH + 5 + s, 8, stride=2), :] for s in range(8)]
            for b in range(7):
                term = dz[0] * row[b] + dz[1] * row[b + 1]
                acc[b] = term if acc[b] is None else acc[b] + term
        rows = [jnp.sum(acc[b], axis=0, keepdims=True) for b in range(7)]
        rows.append(jnp.zeros((1, 128), F32))
        small[layer, pl.ds(pl.multiple_of(a * 8, 8), 8), col] = jnp.concatenate(rows, axis=0)
        return carry

    lax.fori_loop(0, GROUPS * 7, step, 0)


def kernel(
    act_hbm,
    gout_hbm,
    kern_hbm,
    gain_ref,
    shift_ref,
    win_hbm,
    bin_ref,
    wout_hbm,
    gin_ref,
    gk_ref,
    gg_ref,
    gs_ref,
    gb_ref,
    gwi_ref,
    gwo_ref,
    act_ref,
    kern_ref,
    win,
    wout,
    pads,
    z_ref,
    hat_ref,
    inv_ref,
    hid_ref,
    gn_ref,
    slope_ref,
    ga_ref,
    pre_ref,
    dn_ref,
    db_ref,
    red_ref,
    hsend,
    hrecv,
    csend,
    crecv,
    s0,
    r0,
    s1,
    r1,
    own1,
    s2,
    r2,
    own2,
    s3,
    r3,
    fsend,
    frecv,
    small,
    smc,
    smt,
    sma,
    smb,
    smz,
    smg,
    smx,
    wsem,
    hs,
    hr,
    cs,
    cr,
    p0s,
    p0r,
    p1s,
    p1r,
    p2s,
    p2r,
    p3s,
    p3r,
    fs,
    fr,
    mcs,
    mcr,
    mas,
    mar,
    mbs,
    mbr,
    mzs,
    mzr,
    mgs,
    mgr,
    mxs,
    mxr,
):
    r = lax.axis_index("rows")
    c = lax.axis_index("cols")
    y, zl = r // 4, r % 4
    x, zh, core = c // 4, (c // 2) % 2, c % 2
    z = zh * 4 + zl
    first = y * (1 - core) + x * core
    second = x * (1 - core) + y * core
    scale = 1.0 / math.sqrt(256 * 256)

    def device(dx, dy, dz, dcore):
        return (dy * 4 + dz % 4, dx * 4 + (dz // 4) * 2 + dcore)

    def first_peer(k):
        q = (first + k) % 4
        return device(x * (1 - core) + q * core, q * (1 - core) + y * core, z, core)

    def second_peer(k):
        q = (second + k) % 4
        return device(q * (1 - core) + x * core, y * (1 - core) + q * core, z, core)

    def z_peer(k):
        return device(x, y, (z + k) % 8, core)

    def last_target(q):
        return device(q // 2, first, (q % 2) * 4 + second, core)

    def last_source(zs):
        return device(zl * (1 - core) + y * core, y * (1 - core) + zl * core, zs, core)

    partner = (r, c + 1 - 2 * core)

    def is_me(dev):
        return jnp.logical_and(dev[0] == r, dev[1] == c)

    def exists(d):
        rr, cc = r + d[0], c + d[1]
        return jnp.logical_and(
            jnp.logical_and(rr >= 0, rr < 16), jnp.logical_and(cc >= 0, cc < 16)
        )

    act_copy = pltpu.make_async_copy(act_hbm, act_ref, wsem.at[4])
    act_copy.start()
    kern_copy = pltpu.make_async_copy(kern_hbm, kern_ref, wsem.at[5])
    gout_copy = pltpu.make_async_copy(gout_hbm, gn_ref.at[1, 1], wsem.at[6])
    kern_copy.start()
    gout_copy.start()

    barrier = pltpu.get_barrier_semaphore()

    def greet(dev):
        pl.semaphore_signal(barrier, inc=1, device_id=dev, device_id_type=MESH)

    count = jnp.int32(13)
    for d in DIRS:
        ok = exists(d)

        @pl.when(ok)
        def _(d=d):
            greet((r + d[0], c + d[1]))

        count = count + ok.astype(jnp.int32)
    for k in range(1, 4):
        greet(first_peer(k))
        greet(second_peer(k))
    for k in range(1, 8):
        greet(z_peer(k))
    for q in range(8):
        for dev in (last_target(q), last_source(q)):
            away = jnp.logical_not(is_me(dev))

            @pl.when(away)
            def _(dev=dev):
                greet(dev)

            count = count + away.astype(jnp.int32)

    weight_copies = []
    for n, (src, dst, l) in enumerate(
        ((win_hbm, win, 0), (wout_hbm, wout, 0), (win_hbm, win, 1), (wout_hbm, wout, 1))
    ):
        copy = pltpu.make_async_copy(src.at[l], dst.at[l], wsem.at[n])
        copy.start()
        weight_copies.append(copy)

    zero = jnp.zeros((PITCH, 128), F32)

    def clear(it, carry):
        for p in range(4):
            for g in range(GROUPS):
                pads[p, g, pl.ds(pl.multiple_of(it * PITCH, PITCH), PITCH), :] = zero
        return carry

    lax.fori_loop(0, PROWS, clear, 0)
    act_copy.wait()

    def fill(it, carry):
        rows = pl.ds(pl.multiple_of(it * TILE, TILE), TILE)
        for g in range(GROUPS):
            pads[0, g, pl.ds(pl.multiple_of(pad_row(it), 8), TILE), :] = act_ref[
                rows, lanes(g)
            ].astype(F32)
        return carry

    lax.fori_loop(0, TILE, fill, 0)

    def halo_copy(e, n):
        d = DIRS[n]
        size = 32 if d[0] != 0 and d[1] != 0 else 48
        return pltpu.make_async_remote_copy(
            src_ref=hsend.at[e, n, pl.ds(0, size)],
            dst_ref=hrecv.at[e, 7 - n, pl.ds(0, size)],
            send_sem=hs.at[e, n],
            recv_sem=hr.at[e, 7 - n],
            device_id=(r + d[0], c + d[1]),
            device_id_type=MESH,
        )

    def halo_start(e, p):
        for n, d in enumerate(DIRS):
            row0 = {-1: 0, 0: 0, 1: TILE - 3}[d[0]]
            for g in range(GROUPS):
                if d[1] == 0:
                    for k in range(3):
                        hsend[e, n, pl.ds(k * 16, 16), lanes(g)] = pads[
                            p, g, pl.ds(pad_row(row0 + k), TILE), :
                        ].astype(BF16)
                elif d[0] == 0:
                    col0 = 0 if d[1] < 0 else TILE - 3
                    for k in range(3):
                        hsend[e, n, pl.ds(k * 16, 16), lanes(g)] = pads[
                            p, g, pl.ds(pad_row(0) + col0 + k, TILE, stride=PITCH), :
                        ].astype(BF16)
                else:
                    col0 = 0 if d[1] < 0 else 8
                    parts = [
                        pads[p, g, pl.ds(pad_row(row0 + k) + col0, 8), :] for k in range(3)
                    ]
                    hsend[e, n, pl.ds(0, 32), lanes(g)] = jnp.concatenate(
                        parts + [parts[2]], axis=0
                    ).astype(BF16)

            @pl.when(exists(d))
            def _(n=n):
                halo_copy(e, n).start()

    def halo_finish(e, p):
        for n, d in enumerate(DIRS):

            @pl.when(exists(d))
            def _(n=n, d=d):
                size = 32 if d[0] != 0 and d[1] != 0 else 48
                pltpu.make_async_remote_copy(
                    src_ref=hsend.at[e, n, pl.ds(0, size)],
                    dst_ref=hrecv.at[e, n, pl.ds(0, size)],
                    send_sem=hs.at[e, n],
                    recv_sem=hr.at[e, n],
                    device_id=(r + d[0], c + d[1]),
                    device_id_type=MESH,
                ).wait_recv()
                row0 = {-1: -3, 0: 0, 1: TILE}[d[0]]
                for g in range(GROUPS):
                    got = hrecv[e, n, pl.ds(0, size), lanes(g)].astype(F32)
                    if d[1] == 0:
                        for k in range(3):
                            pads[p, g, pl.ds(pad_row(row0 + k), TILE), :] = got[
                                k * 16 : k * 16 + 16
                            ]
                    elif d[0] == 0:
                        col0 = -3 if d[1] < 0 else TILE
                        for k in range(3):
                            pads[
                                p, g, pl.ds(pad_row(0) + col0 + k, TILE, stride=PITCH), :
                            ] = got[k * 16 : k * 16 + 16]
                    else:
                        col0 = -8 if d[1] < 0 else TILE
                        for k in range(3):
                            pads[p, g, pl.ds(pad_row(row0 + k) + col0, 8), :] = got[
                                k * 8 : k * 8 + 8
                            ]

    pl.semaphore_wait(barrier, count)
    halo_start(0, 0)
    kern_copy.wait()

    def forward_norm(layer, p):
        def emit(g, i, par, value):
            z_ref[g, pl.ds(i * TILE + par, 8, stride=2), :] = value

        conv_into(pads.at[p], kern_ref, layer, False, emit)

        def step(it, carry):
            rows = pl.ds(pl.multiple_of(it * 32, 32), 32)
            zs = [z_ref[g, rows, :] for g in range(GROUPS)]
            mean = jnp.sum(zs[0] + zs[1] + zs[2], axis=-1, keepdims=True) * (1.0 / C)
            cen = [v - mean for v in zs]
            var = jnp.sum(
                cen[0] * cen[0] + cen[1] * cen[1] + cen[2] * cen[2], axis=-1, keepdims=True
            ) * (1.0 / C)
            inv = lax.rsqrt(var + EPSILON)
            inv_ref[layer, rows, :] = jnp.broadcast_to(inv, (32, 128))
            for g in range(GROUPS):
                hat = cen[g] * inv
                hat_ref[layer, g, rows, :] = hat
                gn_ref[layer, 0, rows, lanes(g)] = (
                    hat * gain_ref[pl.ds(layer, 1), lanes(g)]
                    + shift_ref[pl.ds(layer, 1), lanes(g)]
                ).astype(BF16)
            return carry

        lax.fori_loop(0, PIX // 32, step, 0)

    def hidden_forward(layer):
        def step(n, carry):
            cols = pl.ds(pl.multiple_of(n * CHUNK, CHUNK), CHUNK)
            pre_ref[...] = jnp.dot(
                gn_ref[layer, 0], win[layer, :, cols], preferred_element_type=F32
            )
            bias = bin_ref[pl.ds(layer, 1), cols]

            def inner(it, carry):
                rows = pl.ds(pl.multiple_of(it * 32, 32), 32)
                act, slope = gelu_parts(pre_ref[rows, :] + bias)
                hid_ref[layer, 1, rows, cols] = act.astype(BF16)
                slope_ref[layer, rows, cols] = slope
                return carry

            lax.fori_loop(0, PIX // 32, inner, 0)
            return carry

        lax.fori_loop(0, HID // CHUNK, step, 0)

    def hidden_grad(layer):
        def step(n, carry):
            cols = pl.ds(pl.multiple_of(n * CHUNK, CHUNK), CHUNK)
            ga_ref[:, cols] = jnp.dot(
                gn_ref[layer, 1], wout[layer, :, cols], preferred_element_type=F32
            )
            return carry

        lax.fori_loop(0, HID // CHUNK, step, 0)

    def slope_times(layer):
        def step(n, carry):
            cols = pl.ds(pl.multiple_of(n * CHUNK, CHUNK), CHUNK)

            def inner(it, total):
                rows = pl.ds(pl.multiple_of(it * 32, 32), 32)
                grad = ga_ref[rows, cols] * slope_ref[layer, rows, cols]
                hid_ref[layer, 0, rows, cols] = grad.astype(BF16)
                return total + (grad[0:8] + grad[8:16]) + (grad[16:24] + grad[24:32])

            total = lax.fori_loop(0, PIX // 32, inner, jnp.zeros((8, CHUNK), F32))
            db_ref[pl.ds(layer, 1), cols] = jnp.sum(total, axis=0, keepdims=True)
            return carry

        lax.fori_loop(0, HID // CHUNK, step, 0)

    def norm_grad(layer, p):
        dn_ref[...] = lax.dot_general(
            hid_ref[layer, 0], win[layer], NT, preferred_element_type=F32
        )
        red_ref[...] = jnp.zeros_like(red_ref)

        def step(it, carry):
            rows = pl.ds(pl.multiple_of(it * 32, 32), 32)
            dn = [dn_ref[rows, lanes(g)] for g in range(GROUPS)]
            hat = [hat_ref[layer, g, rows, :] for g in range(GROUPS)]
            sc = [dn[g] * gain_ref[pl.ds(layer, 1), lanes(g)] for g in range(GROUPS)]
            m1 = jnp.sum(sc[0] + sc[1] + sc[2], axis=-1, keepdims=True) * (1.0 / C)
            m2 = jnp.sum(
                sc[0] * hat[0] + sc[1] * hat[1] + sc[2] * hat[2], axis=-1, keepdims=True
            ) * (1.0 / C)
            inv = inv_ref[layer, rows, :]
            for g in range(GROUPS):
                dz = (inv * (sc[g] - m1 - hat[g] * m2)).astype(BF16).astype(F32)
                for k in range(2):
                    pads[
                        p, g, pl.ds(pl.multiple_of(pad_row(it * 2 + k), 8), TILE), :
                    ] = dz[k * TILE : (k + 1) * TILE]
                prod = dn[g] * hat[g]
                red_ref[0, :, lanes(g)] += (prod[0:8] + prod[8:16]) + (prod[16:24] + prod[24:32])
                red_ref[1, :, lanes(g)] += (dn[g][0:8] + dn[g][8:16]) + (
                    dn[g][16:24] + dn[g][24:32]
                )
            return carry

        lax.fori_loop(0, PIX // 32, step, 0)
        small[layer, pl.ds(56, 1), :] = jnp.sum(red_ref[0], axis=0, keepdims=True)
        small[layer, pl.ds(57, 1), :] = jnp.sum(red_ref[1], axis=0, keepdims=True)
        for k in range(4):
            small[layer, pl.ds(58 + k, 1), :] = db_ref[pl.ds(layer, 1), pl.ds(k * C, C)]
        small[layer, pl.ds(62, 2), :] = jnp.zeros((2, C), F32)

    def remote(src, dst, ssem, rsem, dev):
        return pltpu.make_async_remote_copy(
            src_ref=src,
            dst_ref=dst,
            send_sem=ssem,
            recv_sem=rsem,
            device_id=dev,
            device_id_type=MESH,
        )

    def pair_copy(l, q):
        return remote(csend.at[l, q], crecv.at[l, q], cs.at[l, q], cr.at[l, q], partner)

    def relay_copy(l, k):
        return remote(
            s0.at[l, pl.ds(192 * k, 192)], r0.at[l, k], p0s.at[l, k], p0r.at[l, k], first_peer(1 + 2 * k)
        )

    def first_copy(l, k):
        return remote(s1.at[l, k], r1.at[l, k], p1s.at[l, k], p1r.at[l, k], first_peer(1 + 2 * k))

    def second_copy(l, k):
        return remote(
            s2.at[l, k - 1], r2.at[l, k - 1], p2s.at[l, k - 1], p2r.at[l, k - 1], second_peer(k)
        )

    def last_copy(l, q):
        return remote(s3.at[l, q], r3.at[l, z], p3s.at[l, q], p3r.at[l, z], last_target(q))

    def back_copy(l):
        return remote(fsend.at[l], frecv.at[l], fs.at[l], fr.at[l], partner)

    def weight_grad(l, m, q):
        return lax.dot_general(
            hid_ref[l, m, :, pl.ds(pl.multiple_of(q * C, C), C)],
            gn_ref[l, m],
            TN,
            preferred_element_type=F32,
        )

    def reduce_start(l):
        def away(q, carry):
            csend[l, q] = weight_grad(l, 1 - core, q).astype(BF16)
            pair_copy(l, q).start()
            return carry

        lax.fori_loop(0, 4, away, 0)

    def pair_block(l, k):
        q = (first + k) % 4
        mine = weight_grad(l, core, q)
        pair_copy(l, q).wait_recv()
        return mine + crecv[l, q].astype(F32)

    def reduce_relay(l):
        s0[l] = pair_block(l, 2).astype(BF16)
        for k in range(2):
            relay_copy(l, k).start()

    def reduce_pair(l):
        def step(i, carry):
            own1[l, i] = pair_block(l, 1 + 2 * i)
            return carry

        lax.fori_loop(0, 2, step, 0)
        own1[l, 2] = pair_block(l, 0)

    def reduce_first(l):
        for k in range(2):
            relay_copy(l, k).wait_recv()
            part = pl.ds(192 * k, 192)
            rest = pl.ds(192 * (1 - k), 192)
            s1[l, k, part, :] = (own1[l, k, part, :] + r0[l, k].astype(F32)).astype(BF16)
            s1[l, k, rest, :] = own1[l, k, rest, :].astype(BF16)
            first_copy(l, k).start()

    def reduce_second(l):
        for k in range(2):
            first_copy(l, k).wait_recv()

        def block(k):
            rows = pl.ds(pl.multiple_of(((second + k) % 4) * 96, 96), 96)
            return (
                own1[l, 2, rows, :]
                + r1[l, 0, rows, :].astype(F32)
                + r1[l, 1, rows, :].astype(F32)
            )

        def step(k, carry):
            s2[l, k - 1] = block(k).astype(BF16)
            second_copy(l, k).start()
            return carry

        lax.fori_loop(1, 4, step, 0)
        own2[...] = block(0)

    def reduce_last(l):
        for k in range(1, 4):
            second_copy(l, k).wait_recv()
        total = (
            own2[...]
            + r2[l, 0].astype(F32)
            + r2[l, 1].astype(F32)
            + r2[l, 2].astype(F32)
        )
        pad = jnp.zeros((4, C), F32)
        for q in range(8):
            s3[l, q] = jnp.concatenate([total[12 * q : 12 * q + 12], pad], axis=0).astype(BF16)
            me = is_me(last_target(q))

            @pl.when(jnp.logical_not(me))
            def _(q=q):
                last_copy(l, q).start()

            @pl.when(me)
            def _(q=q):
                r3[l, z] = s3[l, q]

    def reduce_back(l):
        for q in range(8):

            @pl.when(jnp.logical_not(is_me(last_source(q))))
            def _(q=q):
                remote(
                    s3.at[l, 0], r3.at[l, q], p3s.at[l, 0], p3r.at[l, q], last_source(q)
                ).wait_recv()

        total = r3[l, 0].astype(F32)
        for q in range(1, 8):
            total = total + r3[l, q].astype(F32)
        total = total * scale
        pad = jnp.zeros((2, C), F32)
        low = jnp.concatenate([total[0:6], pad], axis=0)
        high = jnp.concatenate([total[6:12], pad], axis=0)
        zeroth = core == 0
        fsend[l] = jnp.where(zeroth, high, low)
        back_copy(l).start()
        return jnp.where(zeroth, low, high)

    def reduce_end(l, mine):
        back_copy(l).wait_recv()
        other = frecv[l]
        zeroth = core == 0
        wi = jnp.where(zeroth, mine, other)
        wo = jnp.where(zeroth, other, mine)
        for j in range(6):
            gwi_ref[j, pl.ds(l, 1), :] = wi[j : j + 1]
            gwo_ref[j, pl.ds(l, 1), :] = wo[j : j + 1]

    def small_pair(l):
        half = pl.ds(pl.multiple_of((1 - core) * 32, 32), 32)
        return remote(small.at[l, half], smc.at[l], mcs.at[l], mcr.at[l], partner)

    def small_first(l, k):
        q = (first + k) % 4
        return remote(
            smt.at[l, q], sma.at[l, k - 1], mas.at[l, k - 1], mar.at[l, k - 1], first_peer(k)
        )

    def small_second(l, k):
        return remote(
            smb.at[l, second],
            smb.at[l, second],
            mbs.at[l, k - 1],
            mbr.at[l, k - 1],
            second_peer(k),
        )

    def small_z(l, k):
        return remote(
            smz.at[l, z], smz.at[l, z], mzs.at[l, k - 1], mzr.at[l, k - 1], z_peer(k)
        )

    def small_gather(l, k):
        return remote(
            smg.at[l, first], smg.at[l, first], mgs.at[l, k - 1], mgr.at[l, k - 1], first_peer(k)
        )

    def small_back(l):
        return remote(smg.at[l], smx.at[l], mxs.at[l], mxr.at[l], partner)

    def small_0(l):
        small_pair(l).start()

    def small_1(l):
        small_pair(l).wait_recv()
        for q in range(4):
            rows = pl.ds(pl.multiple_of(core * 32 + q * 8, 8), 8)
            smt[l, q] = small[l, rows, :] + smc[l, pl.ds(q * 8, 8), :]
        for k in range(1, 4):
            small_first(l, k).start()

    def small_2(l):
        for k in range(1, 4):
            small_first(l, k).wait_recv()
        smb[l, second] = (smt[l, first] + sma[l, 0]) + (sma[l, 1] + sma[l, 2])
        for k in range(1, 4):
            small_second(l, k).start()

    def small_3(l):
        for k in range(1, 4):
            small_second(l, k).wait_recv()
        smz[l, z] = (smb[l, 0] + smb[l, 1]) + (smb[l, 2] + smb[l, 3])
        for k in range(1, 8):
            small_z(l, k).start()

    def small_4(l):
        for k in range(1, 8):
            small_z(l, k).wait_recv()
        total = smz[l, 0]
        for q in range(1, 8):
            total = total + smz[l, q]
        smg[l, first] = total * scale
        for k in range(1, 4):
            small_gather(l, k).start()

    def small_5(l):
        for k in range(1, 4):
            small_gather(l, k).wait_recv()
        small_back(l).start()

    def small_6(l):
        small_back(l).wait_recv()
        zeroth = core == 0
        low = [jnp.where(zeroth, smg[l, q], smx[l, q]) for q in range(4)]
        high = [jnp.where(zeroth, smx[l, q], smg[l, q]) for q in range(4)]
        full = jnp.concatenate(low + high, axis=0)
        for a in range(7):
            for b in range(7):
                gk_ref[a, b, pl.ds(l, 1), :] = full[a * 8 + b : a * 8 + b + 1]
        gg_ref[pl.ds(l, 1), :] = full[56:57]
        gs_ref[pl.ds(l, 1), :] = full[57:58]
        for k in range(4):
            gb_ref[pl.ds(l, 1), pl.ds(k * C, C)] = full[58 + k : 59 + k]

    halo_finish(0, 0)
    forward_norm(0, 0)
    for copy in weight_copies:
        copy.wait()
    hidden_forward(0)
    dn_ref[...] = lax.dot_general(hid_ref[0, 1], wout[0], NT, preferred_element_type=F32)

    def to_middle(it, carry):
        rows = pl.ds(pl.multiple_of(it * TILE, TILE), TILE)
        at = pl.ds(pl.multiple_of(pad_row(it), 8), TILE)
        for g in range(GROUPS):
            pads[1, g, at, :] = (pads[0, g, at, :] + dn_ref[rows, lanes(g)]).astype(BF16).astype(F32)
        return carry

    lax.fori_loop(0, TILE, to_middle, 0)
    halo_start(1, 1)
    gout_copy.wait()
    hidden_grad(1)
    halo_finish(1, 1)
    forward_norm(1, 1)
    hidden_forward(1)
    slope_times(1)
    norm_grad(1, 2)
    halo_start(2, 2)
    taps_grad(pads.at[2], pads.at[1], small, 1)
    small_0(1)
    reduce_start(1)
    small_1(1)
    reduce_relay(1)
    reduce_pair(1)
    halo_finish(2, 2)

    def emit_mid(g, i, par, value):
        z_ref[g, pl.ds(i * TILE + par, 8, stride=2), :] = value

    conv_into(pads.at[2], kern_ref, 1, True, emit_mid)

    def to_grad_mid(it, carry):
        rows = pl.ds(pl.multiple_of(it * 32, 32), 32)
        for g in range(GROUPS):
            gn_ref[0, 1, rows, lanes(g)] = (
                gn_ref[1, 1, rows, lanes(g)].astype(F32) + z_ref[g, rows, :]
            ).astype(BF16)
        return carry

    lax.fori_loop(0, PIX // 32, to_grad_mid, 0)
    small_2(1)
    reduce_first(1)
    hidden_grad(0)
    slope_times(0)
    reduce_start(0)
    norm_grad(0, 3)
    halo_start(3, 3)
    small_3(1)
    reduce_relay(0)
    taps_grad(pads.at[3], pads.at[0], small, 0)
    small_0(0)
    reduce_pair(0)
    small_1(0)
    reduce_second(1)
    reduce_first(0)
    small_4(1)
    halo_finish(3, 3)
    small_2(0)
    conv_into(pads.at[3], kern_ref, 0, True, emit_mid)

    def to_grad_in(it, carry):
        rows = pl.ds(pl.multiple_of(it * 32, 32), 32)
        for g in range(GROUPS):
            gin_ref[rows, lanes(g)] = (
                gn_ref[0, 1, rows, lanes(g)].astype(F32) + z_ref[g, rows, :]
            ).astype(BF16)
        return carry

    lax.fori_loop(0, PIX // 32, to_grad_in, 0)
    small_3(0)
    reduce_last(1)
    small_5(1)
    reduce_second(0)
    small_4(0)
    mine_1 = reduce_back(1)
    small_6(1)
    reduce_last(0)
    small_5(0)
    reduce_end(1, mine_1)
    small_6(0)
    mine_0 = reduce_back(0)
    reduce_end(0, mine_0)

    for e in range(4):
        for n, d in enumerate(DIRS):

            @pl.when(exists(d))
            def _(e=e, n=n):
                halo_copy(e, n).wait_send()

    for l in range(2):
        for q in range(4):
            pair_copy(l, q).wait_send()
        for k in range(2):
            relay_copy(l, k).wait_send()
            first_copy(l, k).wait_send()
        for k in range(1, 4):
            second_copy(l, k).wait_send()
            small_first(l, k).wait_send()
            small_second(l, k).wait_send()
            small_gather(l, k).wait_send()
        for k in range(1, 8):
            small_z(l, k).wait_send()
        for q in range(8):

            @pl.when(jnp.logical_not(is_me(last_target(q))))
            def _(l=l, q=q):
                last_copy(l, q).wait_send()

        back_copy(l).wait_send()
        small_pair(l).wait_send()
        small_back(l).wait_send()


def hand_over(*refs):
    half = len(refs) // 2
    for src, dst in zip(refs[:half], refs[half:]):
        dst[...] = src[...]


def shards(activations, grad_out, kernels, norm_gains, norm_shifts, w_in, b_in, w_out):
    vmem = pl.BlockSpec(memory_space=pltpu.VMEM)
    hbm = pl.BlockSpec(memory_space=pl.ANY)
    dma = pltpu.SemaphoreType.DMA
    pad_size = PROWS * PITCH
    scratch = [
        pltpu.VMEM((PIX, C), BF16),
        pltpu.VMEM((7, 7, 2, C), F32),
        pltpu.VMEM((2, C, HID), BF16),
        pltpu.VMEM((2, C, HID), BF16),
        pltpu.VMEM((4, GROUPS, pad_size, 128), F32),
        pltpu.VMEM((GROUPS, PIX, 128), F32),
        pltpu.VMEM((2, GROUPS, PIX, 128), F32),
        pltpu.VMEM((2, PIX, 128), F32),
        pltpu.VMEM((2, 2, PIX, HID), BF16),
        pltpu.VMEM((2, 2, PIX, C), BF16),
        pltpu.VMEM((2, PIX, HID), F32),
        pltpu.VMEM((PIX, HID), F32),
        pltpu.VMEM((PIX, CHUNK), F32),
        pltpu.VMEM((PIX, C), F32),
        pltpu.VMEM((2, HID), F32),
        pltpu.VMEM((2, 8, C), F32),
        pltpu.VMEM((4, 8, 48, C), BF16),
        pltpu.VMEM((4, 8, 48, C), BF16),
        pltpu.VMEM((2, 4, C, C), BF16),
        pltpu.VMEM((2, 4, C, C), BF16),
        pltpu.VMEM((2, C, C), BF16),
        pltpu.VMEM((2, 2, C // 2, C), BF16),
        pltpu.VMEM((2, 2, C, C), BF16),
        pltpu.VMEM((2, 2, C, C), BF16),
        pltpu.VMEM((2, 3, C, C), F32),
        pltpu.VMEM((2, 3, 96, C), BF16),
        pltpu.VMEM((2, 3, 96, C), BF16),
        pltpu.VMEM((96, C), F32),
        pltpu.VMEM((2, 8, 16, C), BF16),
        pltpu.VMEM((2, 8, 16, C), BF16),
        pltpu.VMEM((2, 8, C), F32),
        pltpu.VMEM((2, 8, C), F32),
        pltpu.VMEM((2, SMALL, C), F32),
        pltpu.VMEM((2, 32, C), F32),
        pltpu.VMEM((2, 4, 8, C), F32),
        pltpu.VMEM((2, 3, 8, C), F32),
        pltpu.VMEM((2, 4, 8, C), F32),
        pltpu.VMEM((2, 8, 8, C), F32),
        pltpu.VMEM((2, 4, 8, C), F32),
        pltpu.VMEM((2, 4, 8, C), F32),
        dma((7,)),
        dma((4, 8)),
        dma((4, 8)),
        dma((2, 4)),
        dma((2, 4)),
        dma((2, 2)),
        dma((2, 2)),
        dma((2, 2)),
        dma((2, 2)),
        dma((2, 3)),
        dma((2, 3)),
        dma((2, 8)),
        dma((2, 8)),
        dma((2,)),
        dma((2,)),
        dma((2,)),
        dma((2,)),
        dma((2, 3)),
        dma((2, 3)),
        dma((2, 3)),
        dma((2, 3)),
        dma((2, 7)),
        dma((2, 7)),
        dma((2, 3)),
        dma((2, 3)),
        dma((2,)),
        dma((2,)),
    ]
    sds = jax.ShapeDtypeStruct
    outs = pl.pallas_call(
        kernel,
        out_shape=(
            sds((PIX, C), BF16),
            sds((7, 7, 2, C), F32),
            sds((2, C), F32),
            sds((2, C), F32),
            sds((2, HID), F32),
            sds((6, 2, C), F32),
            sds((6, 2, C), F32),
        ),
        in_specs=[hbm, hbm, hbm, vmem, vmem, hbm, vmem, hbm],
        out_specs=(vmem,) * 7,
        scratch_shapes=scratch,
        compiler_params=pltpu.CompilerParams(
            collective_id=0, has_side_effects=True, vmem_limit_bytes=64000000
        ),
        name="convnext_step",
    )(
        activations.reshape(PIX, C),
        grad_out.reshape(PIX, C),
        jnp.transpose(kernels, (1, 2, 0, 3)),
        norm_gains,
        norm_shifts,
        w_in,
        b_in,
        w_out,
    )
    grad_in, gk, gg, gs, gb, gwi, gwo = pl.pallas_call(
        hand_over,
        out_shape=tuple(sds(o.shape, o.dtype) for o in outs),
        in_specs=[vmem] * 7,
        out_specs=(vmem,) * 7,
        name="hand_over",
    )(*outs)
    return (
        grad_in.reshape(activations.shape),
        jnp.transpose(gk, (2, 0, 1, 3)),
        gg,
        gs,
        gb,
        jnp.transpose(gwi, (1, 2, 0)),
        jnp.transpose(gwo, (1, 2, 0)),
    )


def solution(mesh):
    return jax.shard_map(
        shards,
        mesh=mesh,
        in_specs=(P("rows", "cols", None), P("rows", "cols", None), P(), P(), P(), P(), P(), P()),
        out_specs=(
            P("rows", "cols", None),
            P(),
            P(),
            P(),
            P(),
            P(None, None, ("rows", "cols")),
            P(None, None, ("rows", "cols")),
        ),
        check_vma=False,
    )
```

```python
import functools
import math

import jax
import jax.numpy as jnp
from jax import lax
from jax.experimental import pallas as pl
from jax.experimental.pallas import tpu as pltpu
from jax.sharding import PartitionSpec as P

EPSILON = 1e-06
ROOT_HALF = 0.7071067811865476
INV_ROOT_TAU = 0.3989422804014327
MESH = pl.DeviceIdType.MESH
F32 = jnp.float32
BF16 = jnp.bfloat16

C = 384
HID = 1536
TILE = 16
PIX = TILE * TILE
PITCH = 32
PROWS = TILE + 6
GROUPS = C // 128
CHUNK = 256
SMALL = 64
DIRS = tuple((dr, dc) for dr in (-1, 0, 1) for dc in (-1, 0, 1) if (dr, dc) != (0, 0))
TN = (((0,), (0,)), ((), ()))
NT = (((1,), (1,)), ((), ()))


def lanes(g):
    return pl.ds(g * 128, 128)


def gelu_parts(pre):
    cdf = 0.5 * (1.0 + lax.erf(pre * ROOT_HALF))
    density = jnp.exp(-0.5 * pre * pre) * INV_ROOT_TAU
    return pre * cdf, cdf + pre * density


def pad_row(i):
    return (i + 3) * PITCH + 8


def conv_into(src, kern, layer, flip, emit):
    block = 4

    def step(it, carry):
        g = it // (TILE // block)
        row = (it % (TILE // block)) * block
        col = pl.ds(pl.multiple_of(g * 128, 128), 128)
        acc = [[None, None] for _ in range(block)]
        for rho in range(block + 6):
            taps = [
                src[g, pl.ds((row + rho) * PITCH + 5 + s, 8, stride=2), :] for s in range(8)
            ]
            for i in range(block):
                a = rho - i
                if a < 0 or a > 6:
                    continue
                for b in range(7):
                    ka, kb = (6 - a, 6 - b) if flip else (a, b)
                    w = kern[ka, kb, pl.ds(layer, 1), col]
                    for par in range(2):
                        term = taps[b + par] * w
                        acc[i][par] = term if acc[i][par] is None else acc[i][par] + term
        for i in range(block):
            for par in range(2):
                emit(g, row + i, par, acc[i][par])
        return carry

    lax.fori_loop(0, GROUPS * (TILE // block), step, 0)


def taps_grad(grad, src, small, layer):
    def step(it, carry):
        g = it // 7
        a = it % 7
        col = pl.ds(pl.multiple_of(g * 128, 128), 128)
        acc = [None] * 7
        for i in range(TILE):
            dz = [grad[g, pl.ds(pad_row(i) + par, 8, stride=2), :] for par in range(2)]
            row = [src[g, pl.ds((i + a) * PITCH + 5 + s, 8, stride=2), :] for s in range(8)]
            for b in range(7):
                term = dz[0] * row[b] + dz[1] * row[b + 1]
                acc[b] = term if acc[b] is None else acc[b] + term
        rows = [jnp.sum(acc[b], axis=0, keepdims=True) for b in range(7)]
        rows.append(jnp.zeros((1, 128), F32))
        small[layer, pl.ds(pl.multiple_of(a * 8, 8), 8), col] = jnp.concatenate(rows, axis=0)
        return carry

    lax.fori_loop(0, GROUPS * 7, step, 0)


def kernel(
    act_hbm,
    gout_hbm,
    kern_hbm,
    gain_hbm,
    shift_hbm,
    win_hbm,
    bin_hbm,
    wout_hbm,
    gin_hbm,
    gk_hbm,
    gg_hbm,
    gs_hbm,
    gb_hbm,
    gwi_hbm,
    gwo_hbm,
    gin_ref,
    gk_ref,
    gg_ref,
    gs_ref,
    gb_ref,
    gwi_ref,
    gwo_ref,
    gain_ref,
    shift_ref,
    bin_ref,
    act_ref,
    kern_ref,
    win,
    wout,
    pads,
    z_ref,
    hat_ref,
    inv_ref,
    hid_ref,
    gn_ref,
    slope_ref,
    ga_ref,
    pre_ref,
    dn_ref,
    db_ref,
    hsend,
    hrecv,
    csend,
    crecv,
    s0,
    r0,
    s1,
    r1,
    own1,
    s2,
    r2,
    own2,
    s3,
    r3,
    small,
    smc,
    smt,
    sma,
    smb,
    smz,
    smg,
    smx,
    wsem,
    hs,
    hr,
    cs,
    cr,
    p0s,
    p0r,
    p1s,
    p1r,
    p2s,
    p2r,
    p3s,
    p3r,
    mcs,
    mcr,
    mas,
    mar,
    mbs,
    mbr,
    mzs,
    mzr,
    mgs,
    mgr,
    mxs,
    mxr,
):
    r = lax.axis_index("rows")
    c = lax.axis_index("cols")
    y, zl = r // 4, r % 4
    x, zh, core = c // 4, (c // 2) % 2, c % 2
    z = zh * 4 + zl
    first = y * (1 - core) + x * core
    second = x * (1 - core) + y * core
    scale = 1.0 / math.sqrt(256 * 256)

    def device(dx, dy, dz, dcore):
        return (dy * 4 + dz % 4, dx * 4 + (dz // 4) * 2 + dcore)

    def first_peer(k):
        q = (first + k) % 4
        return device(x * (1 - core) + q * core, q * (1 - core) + y * core, z, core)

    def second_peer(k):
        q = (second + k) % 4
        return device(q * (1 - core) + x * core, y * (1 - core) + q * core, z, core)

    def z_peer(k):
        return device(x, y, (z + k) % 8, core)

    def last_target(q):
        return device(q // 4, first, (q // 2 % 2) * 4 + second, q % 2)

    def last_source(q):
        return device(zl, y, q, 0) if q < 8 else device(y, zl, q - 8, 1)

    partner = (r, c + 1 - 2 * core)

    def is_me(dev):
        return jnp.logical_and(dev[0] == r, dev[1] == c)

    def exists(d):
        rr, cc = r + d[0], c + d[1]
        return jnp.logical_and(
            jnp.logical_and(rr >= 0, rr < 16), jnp.logical_and(cc >= 0, cc < 16)
        )

    act_copy = pltpu.make_async_copy(act_hbm, act_ref, wsem.at[4])
    act_copy.start()
    kern_copy = pltpu.make_async_copy(kern_hbm, kern_ref, wsem.at[5])
    gout_copy = pltpu.make_async_copy(gout_hbm, gn_ref.at[1, 1], wsem.at[6])
    kern_copy.start()
    gout_copy.start()
    vector_copies = [
        pltpu.make_async_copy(src, dst, wsem.at[7 + n])
        for n, (src, dst) in enumerate(
            ((gain_hbm, gain_ref), (shift_hbm, shift_ref), (bin_hbm, bin_ref))
        )
    ]
    for copy in vector_copies:
        copy.start()
    result_copies = [
        pltpu.make_async_copy(src, dst, wsem.at[10 + n])
        for n, (src, dst) in enumerate(
            (
                (gin_ref, gin_hbm),
                (gk_ref, gk_hbm),
                (gg_ref, gg_hbm),
                (gs_ref, gs_hbm),
                (gb_ref, gb_hbm),
                (gwi_ref, gwi_hbm),
                (gwo_ref, gwo_hbm),
            )
        )
    ]

    barrier = pltpu.get_barrier_semaphore()

    def greet(dev):
        pl.semaphore_signal(barrier, inc=1, device_id=dev, device_id_type=MESH)

    count = jnp.int32(13)
    for d in DIRS:
        ok = exists(d)

        @pl.when(ok)
        def _(d=d):
            greet((r + d[0], c + d[1]))

        count = count + ok.astype(jnp.int32)
    for k in range(1, 4):
        greet(first_peer(k))
        greet(second_peer(k))
    for k in range(1, 8):
        greet(z_peer(k))
    for q in range(16):
        for dev in (last_target(q), last_source(q)):
            away = jnp.logical_not(is_me(dev))

            @pl.when(away)
            def _(dev=dev):
                greet(dev)

            count = count + away.astype(jnp.int32)

    weight_copies = []
    for n, (src, dst, l) in enumerate(
        ((win_hbm, win, 0), (wout_hbm, wout, 0), (win_hbm, win, 1), (wout_hbm, wout, 1))
    ):
        copy = pltpu.make_async_copy(src.at[l], dst.at[l], wsem.at[n])
        copy.start()
        weight_copies.append(copy)

    zero = jnp.zeros((PITCH, 128), F32)

    def clear(it, carry):
        for p in range(4):
            for g in range(GROUPS):
                pads[p, g, pl.ds(pl.multiple_of(it * PITCH, PITCH), PITCH), :] = zero
        return carry

    lax.fori_loop(0, PROWS, clear, 0)
    act_copy.wait()

    def fill(it, carry):
        rows = pl.ds(pl.multiple_of(it * TILE, TILE), TILE)
        for g in range(GROUPS):
            pads[0, g, pl.ds(pl.multiple_of(pad_row(it), 8), TILE), :] = act_ref[
                rows, lanes(g)
            ].astype(F32)
        return carry

    lax.fori_loop(0, TILE, fill, 0)

    def halo_copy(e, n):
        d = DIRS[n]
        size = 16 if d[0] != 0 and d[1] != 0 else 48
        return pltpu.make_async_remote_copy(
            src_ref=hsend.at[e, n, pl.ds(0, size)],
            dst_ref=hrecv.at[e, 7 - n, pl.ds(0, size)],
            send_sem=hs.at[e, n],
            recv_sem=hr.at[e, 7 - n],
            device_id=(r + d[0], c + d[1]),
            device_id_type=MESH,
        )

    def halo_start(e, p):
        for n, d in enumerate(DIRS):
            row0 = {-1: 0, 0: 0, 1: TILE - 3}[d[0]]
            for g in range(GROUPS):
                if d[1] == 0:
                    for k in range(3):
                        hsend[e, n, pl.ds(k * 16, 16), lanes(g)] = pads[
                            p, g, pl.ds(pad_row(row0 + k), TILE), :
                        ].astype(BF16)
                elif d[0] == 0:
                    col0 = 0 if d[1] < 0 else TILE - 3
                    for k in range(3):
                        hsend[e, n, pl.ds(k * 16, 16), lanes(g)] = pads[
                            p, g, pl.ds(pad_row(0) + col0 + k, TILE, stride=PITCH), :
                        ].astype(BF16)
                else:
                    col0 = 0 if d[1] < 0 else 8
                    cut = slice(0, 3) if d[1] < 0 else slice(5, 8)
                    parts = [
                        pads[p, g, pl.ds(pad_row(row0 + k) + col0, 8), :] for k in range(3)
                    ]
                    hsend[e, n, pl.ds(0, 16), lanes(g)] = jnp.concatenate(
                        [v[cut] for v in parts] + [parts[0][0:7]], axis=0
                    ).astype(BF16)

            @pl.when(exists(d))
            def _(n=n):
                halo_copy(e, n).start()

    def halo_finish(e, p):
        for n, d in enumerate(DIRS):

            @pl.when(exists(d))
            def _(n=n, d=d):
                size = 16 if d[0] != 0 and d[1] != 0 else 48
                pltpu.make_async_remote_copy(
                    src_ref=hsend.at[e, n, pl.ds(0, size)],
                    dst_ref=hrecv.at[e, n, pl.ds(0, size)],
                    send_sem=hs.at[e, n],
                    recv_sem=hr.at[e, n],
                    device_id=(r + d[0], c + d[1]),
                    device_id_type=MESH,
                ).wait_recv()
                row0 = {-1: -3, 0: 0, 1: TILE}[d[0]]
                for g in range(GROUPS):
                    got = hrecv[e, n, pl.ds(0, size), lanes(g)].astype(F32)
                    if d[1] == 0:
                        for k in range(3):
                            pads[p, g, pl.ds(pad_row(row0 + k), TILE), :] = got[
                                k * 16 : k * 16 + 16
                            ]
                    elif d[0] == 0:
                        col0 = -3 if d[1] < 0 else TILE
                        for k in range(3):
                            pads[
                                p, g, pl.ds(pad_row(0) + col0 + k, TILE, stride=PITCH), :
                            ] = got[k * 16 : k * 16 + 16]
                    else:
                        col0 = -3 if d[1] < 0 else TILE
                        for k in range(3):
                            pads[p, g, pl.ds(pad_row(row0 + k) + col0, 3), :] = got[
                                k * 3 : k * 3 + 3
                            ]

    pl.semaphore_wait(barrier, count)
    halo_start(0, 0)
    kern_copy.wait()
    for copy in vector_copies:
        copy.wait()

    def forward_norm(layer, p):
        def emit(g, i, par, value):
            z_ref[g, pl.ds(i * TILE + par, 8, stride=2), :] = value

        conv_into(pads.at[p], kern_ref, layer, False, emit)

        def step(it, carry):
            rows = pl.ds(pl.multiple_of(it * 32, 32), 32)
            zs = [z_ref[g, rows, :] for g in range(GROUPS)]
            mean = jnp.sum(zs[0] + zs[1] + zs[2], axis=-1, keepdims=True) * (1.0 / C)
            cen = [v - mean for v in zs]
            var = jnp.sum(
                cen[0] * cen[0] + cen[1] * cen[1] + cen[2] * cen[2], axis=-1, keepdims=True
            ) * (1.0 / C)
            inv = lax.rsqrt(var + EPSILON)
            inv_ref[layer, rows, :] = jnp.broadcast_to(inv, (32, 128))
            for g in range(GROUPS):
                hat = cen[g] * inv
                hat_ref[layer, g, rows, :] = hat
                gn_ref[layer, 0, rows, lanes(g)] = (
                    hat * gain_ref[pl.ds(layer, 1), lanes(g)]
                    + shift_ref[pl.ds(layer, 1), lanes(g)]
                ).astype(BF16)
            return carry

        lax.fori_loop(0, PIX // 32, step, 0, unroll=4)

    def hidden_forward(layer):
        steps = HID // CHUNK

        def product(n):
            pre_ref[n % 2] = jnp.dot(
                gn_ref[layer, 0], win[layer, :, n * CHUNK : (n + 1) * CHUNK], preferred_element_type=F32
            )

        product(0)
        for n in range(steps):
            cols = pl.ds(n * CHUNK, CHUNK)
            if n + 1 < steps:
                product(n + 1)
            bias = bin_ref[pl.ds(layer, 1), cols]
            for it in range(PIX // 32):
                rows = pl.ds(it * 32, 32)
                act, slope = gelu_parts(pre_ref[n % 2, rows, :] + bias)
                hid_ref[layer, 1, rows, cols] = act.astype(BF16)
                slope_ref[layer, rows, cols] = slope

    def hidden_grad(layer):
        for n in range(HID // CHUNK):
            cols = pl.ds(n * CHUNK, CHUNK)
            ga_ref[:, cols] = jnp.dot(
                gn_ref[layer, 1], wout[layer, :, cols], preferred_element_type=F32
            )

    def slope_times(layer, matmul):
        steps = HID // CHUNK

        def product(n):
            cols = pl.ds(n * CHUNK, CHUNK)
            ga_ref[:, cols] = jnp.dot(
                gn_ref[layer, 1], wout[layer, :, cols], preferred_element_type=F32
            )

        if matmul:
            product(0)
        for n in range(steps):
            cols = pl.ds(n * CHUNK, CHUNK)
            if matmul and n + 1 < steps:
                product(n + 1)
            total = jnp.zeros((8, CHUNK), F32)
            for it in range(PIX // 32):
                rows = pl.ds(it * 32, 32)
                grad = ga_ref[rows, cols] * slope_ref[layer, rows, cols]
                hid_ref[layer, 0, rows, cols] = grad.astype(BF16)
                total = total + (grad[0:8] + grad[8:16]) + (grad[16:24] + grad[24:32])
            db_ref[pl.ds(layer, 1), cols] = jnp.sum(total, axis=0, keepdims=True)

    def norm_grad(layer, p):
        dn_ref[...] = lax.dot_general(
            hid_ref[layer, 0], win[layer], NT, preferred_element_type=F32
        )

        def step(it, carry):
            carry = list(carry)
            rows = pl.ds(pl.multiple_of(it * 32, 32), 32)
            dn = [dn_ref[rows, lanes(g)] for g in range(GROUPS)]
            hat = [hat_ref[layer, g, rows, :] for g in range(GROUPS)]
            sc = [dn[g] * gain_ref[pl.ds(layer, 1), lanes(g)] for g in range(GROUPS)]
            m1 = jnp.sum(sc[0] + sc[1] + sc[2], axis=-1, keepdims=True) * (1.0 / C)
            m2 = jnp.sum(
                sc[0] * hat[0] + sc[1] * hat[1] + sc[2] * hat[2], axis=-1, keepdims=True
            ) * (1.0 / C)
            inv = inv_ref[layer, rows, :]
            for g in range(GROUPS):
                dz = (inv * (sc[g] - m1 - hat[g] * m2)).astype(BF16).astype(F32)
                for k in range(2):
                    pads[
                        p, g, pl.ds(pl.multiple_of(pad_row(it * 2 + k), 8), TILE), :
                    ] = dz[k * TILE : (k + 1) * TILE]
                prod = dn[g] * hat[g]
                carry[g] += (prod[0:8] + prod[8:16]) + (prod[16:24] + prod[24:32])
                carry[3 + g] += (dn[g][0:8] + dn[g][8:16]) + (dn[g][16:24] + dn[g][24:32])
            return tuple(carry)

        sums = lax.fori_loop(
            0, PIX // 32, step, (jnp.zeros((8, 128), F32),) * 6, unroll=4
        )
        for g in range(GROUPS):
            for k in range(2):
                small[layer, pl.ds(56 + k, 1), lanes(g)] = jnp.sum(
                    sums[3 * k + g], axis=0, keepdims=True
                )
        for k in range(4):
            small[layer, pl.ds(58 + k, 1), :] = db_ref[pl.ds(layer, 1), pl.ds(k * C, C)]
        small[layer, pl.ds(62, 2), :] = jnp.zeros((2, C), F32)

    def remote(src, dst, ssem, rsem, dev):
        return pltpu.make_async_remote_copy(
            src_ref=src,
            dst_ref=dst,
            send_sem=ssem,
            recv_sem=rsem,
            device_id=dev,
            device_id_type=MESH,
        )

    def pair_copy(l, q):
        return remote(csend.at[l, q], crecv.at[l, q], cs.at[l, q], cr.at[l, q], partner)

    def relay_copy(l, k):
        return remote(
            s0.at[l, pl.ds(192 * k, 192)], r0.at[l, k], p0s.at[l, k], p0r.at[l, k], first_peer(1 + 2 * k)
        )

    def first_copy(l, k):
        return remote(s1.at[l, k], r1.at[l, k], p1s.at[l, k], p1r.at[l, k], first_peer(1 + 2 * k))

    def second_copy(l, k):
        return remote(
            s2.at[l, k - 1], r2.at[l, k - 1], p2s.at[l, k - 1], p2r.at[l, k - 1], second_peer(k)
        )

    def last_copy(l, q):
        slot = core * 8 + z
        return remote(s3.at[l, q], r3.at[l, slot], p3s.at[l, q], p3r.at[l, slot], last_target(q))

    def weight_grad(l, m, q):
        return lax.dot_general(
            hid_ref[l, m, :, pl.ds(pl.multiple_of(q * C, C), C)],
            gn_ref[l, m],
            TN,
            preferred_element_type=F32,
        )

    def reduce_start(l):
        for k in (2, 3, 1, 0):
            q = (second + k) % 4
            csend[l, q] = weight_grad(l, 1 - core, q).astype(BF16)
            pair_copy(l, q).start()

    def pair_block(l, k):
        q = (first + k) % 4
        mine = weight_grad(l, core, q)
        pair_copy(l, q).wait_recv()
        return mine + crecv[l, q].astype(F32)

    def reduce_relay(l):
        s0[l] = pair_block(l, 2).astype(BF16)
        for k in range(2):
            relay_copy(l, k).start()

    def reduce_pair(l):
        for i, k in enumerate((3, 1, 0)):
            own1[l, i] = pair_block(l, k)

    def reduce_first(l):
        for k in range(2):
            relay_copy(l, k).wait_recv()
            part = pl.ds(192 * k, 192)
            rest = pl.ds(192 * (1 - k), 192)
            s1[l, k, part, :] = (own1[l, 1 - k, part, :] + r0[l, k].astype(F32)).astype(BF16)
            s1[l, k, rest, :] = own1[l, 1 - k, rest, :].astype(BF16)
            first_copy(l, k).start()

    def reduce_second(l):
        for k in range(2):
            first_copy(l, k).wait_recv()

        def block(k):
            rows = pl.ds(pl.multiple_of(((second + k) % 4) * 96, 96), 96)
            return (
                own1[l, 2, rows, :]
                + r1[l, 0, rows, :].astype(F32)
                + r1[l, 1, rows, :].astype(F32)
            )

        def step(k, carry):
            s2[l, k - 1] = block(k).astype(BF16)
            second_copy(l, k).start()
            return carry

        lax.fori_loop(1, 4, step, 0)
        own2[...] = block(0)

    def reduce_last(l):
        for k in range(1, 4):
            second_copy(l, k).wait_recv()
        total = (
            own2[...]
            + r2[l, 0].astype(F32)
            + r2[l, 1].astype(F32)
            + r2[l, 2].astype(F32)
        )
        for q in range(16):
            piece = total[6 * q : 6 * q + 6]
            s3[l, q] = jnp.concatenate([piece, piece[0:2]], axis=0).astype(BF16)
            me = is_me(last_target(q))

            @pl.when(jnp.logical_not(me))
            def _(q=q):
                last_copy(l, q).start()

            @pl.when(me)
            def _(q=q):
                r3[l, core * 8 + z] = s3[l, q]

    def reduce_end(l):
        for q in range(16):

            @pl.when(jnp.logical_not(is_me(last_source(q))))
            def _(q=q):
                remote(
                    s3.at[l, q], r3.at[l, q], p3s.at[l, q], p3r.at[l, q], last_source(q)
                ).wait_recv()

        for m, out in ((0, gwi_ref), (1, gwo_ref)):
            total = r3[l, 8 * m].astype(F32)
            for q in range(1, 8):
                total = total + r3[l, 8 * m + q].astype(F32)
            total = total * scale
            for j in range(6):
                out[j, pl.ds(l, 1), :] = total[j : j + 1]

    def small_pair(l):
        half = pl.ds(pl.multiple_of((1 - core) * 32, 32), 32)
        return remote(small.at[l, half], smc.at[l], mcs.at[l], mcr.at[l], partner)

    def small_first(l, k):
        q = (first + k) % 4
        return remote(
            smt.at[l, q], sma.at[l, k - 1], mas.at[l, k - 1], mar.at[l, k - 1], first_peer(k)
        )

    def small_second(l, k):
        return remote(
            smb.at[l, second],
            smb.at[l, second],
            mbs.at[l, k - 1],
            mbr.at[l, k - 1],
            second_peer(k),
        )

    def small_z(l, k):
        return remote(
            smz.at[l, z], smz.at[l, z], mzs.at[l, k - 1], mzr.at[l, k - 1], z_peer(k)
        )

    def small_gather(l, k):
        return remote(
            smg.at[l, first], smg.at[l, first], mgs.at[l, k - 1], mgr.at[l, k - 1], first_peer(k)
        )

    def small_back(l):
        return remote(smg.at[l], smx.at[l], mxs.at[l], mxr.at[l], partner)

    def small_0(l):
        small_pair(l).start()

    def small_1(l):
        small_pair(l).wait_recv()
        for q in range(4):
            rows = pl.ds(pl.multiple_of(core * 32 + q * 8, 8), 8)
            smt[l, q] = small[l, rows, :] + smc[l, pl.ds(q * 8, 8), :]
        for k in range(1, 4):
            small_first(l, k).start()

    def small_2(l):
        for k in range(1, 4):
            small_first(l, k).wait_recv()
        total = (smt[l, first] + sma[l, 0]) + (sma[l, 1] + sma[l, 2])
        smb[l, second] = total.astype(BF16)
        for k in range(1, 4):
            small_second(l, k).start()

    def small_3(l):
        for k in range(1, 4):
            small_second(l, k).wait_recv()
        part = [smb[l, q].astype(F32) for q in range(4)]
        smz[l, z] = ((part[0] + part[1]) + (part[2] + part[3])).astype(BF16)
        for k in range(1, 8):
            small_z(l, k).start()

    def small_4(l):
        for k in range(1, 8):
            small_z(l, k).wait_recv()
        total = smz[l, 0].astype(F32)
        for q in range(1, 8):
            total = total + smz[l, q].astype(F32)
        smg[l, first] = total * scale
        for k in range(1, 4):
            small_gather(l, k).start()

    def small_5(l):
        for k in range(1, 4):
            small_gather(l, k).wait_recv()
        small_back(l).start()

    def small_6(l):
        small_back(l).wait_recv()
        zeroth = core == 0
        low = [jnp.where(zeroth, smg[l, q], smx[l, q]) for q in range(4)]
        high = [jnp.where(zeroth, smx[l, q], smg[l, q]) for q in range(4)]
        full = jnp.concatenate(low + high, axis=0)
        for a in range(7):
            for b in range(7):
                gk_ref[a, b, pl.ds(l, 1), :] = full[a * 8 + b : a * 8 + b + 1]
        gg_ref[pl.ds(l, 1), :] = full[56:57]
        gs_ref[pl.ds(l, 1), :] = full[57:58]
        for k in range(4):
            gb_ref[pl.ds(l, 1), pl.ds(k * C, C)] = full[58 + k : 59 + k]

    halo_finish(0, 0)
    forward_norm(0, 0)
    for copy in weight_copies:
        copy.wait()
    hidden_forward(0)
    dn_ref[...] = lax.dot_general(hid_ref[0, 1], wout[0], NT, preferred_element_type=F32)

    def to_middle(it, carry):
        rows = pl.ds(pl.multiple_of(it * TILE, TILE), TILE)
        at = pl.ds(pl.multiple_of(pad_row(it), 8), TILE)
        for g in range(GROUPS):
            pads[1, g, at, :] = (pads[0, g, at, :] + dn_ref[rows, lanes(g)]).astype(BF16).astype(F32)
        return carry

    lax.fori_loop(0, TILE, to_middle, 0)
    halo_start(1, 1)
    gout_copy.wait()
    hidden_grad(1)
    halo_finish(1, 1)
    forward_norm(1, 1)
    hidden_forward(1)
    slope_times(1, False)
    norm_grad(1, 2)
    halo_start(2, 2)
    taps_grad(pads.at[2], pads.at[1], small, 1)
    small_0(1)
    reduce_start(1)
    reduce_relay(1)
    small_1(1)
    reduce_pair(1)
    halo_finish(2, 2)

    def emit_mid(g, i, par, value):
        z_ref[g, pl.ds(i * TILE + par, 8, stride=2), :] = value

    conv_into(pads.at[2], kern_ref, 1, True, emit_mid)

    def to_grad_mid(it, carry):
        rows = pl.ds(pl.multiple_of(it * 32, 32), 32)
        for g in range(GROUPS):
            gn_ref[0, 1, rows, lanes(g)] = (
                gn_ref[1, 1, rows, lanes(g)].astype(F32) + z_ref[g, rows, :]
            ).astype(BF16)
        return carry

    lax.fori_loop(0, PIX // 32, to_grad_mid, 0)
    slope_times(0, True)
    reduce_first(1)
    reduce_start(0)
    norm_grad(0, 3)
    halo_start(3, 3)
    reduce_relay(0)
    taps_grad(pads.at[3], pads.at[0], small, 0)
    small_0(0)
    small_2(1)
    reduce_pair(0)
    small_1(0)
    reduce_first(0)
    reduce_second(1)
    small_3(1)
    halo_finish(3, 3)
    small_2(0)
    conv_into(pads.at[3], kern_ref, 0, True, emit_mid)

    def to_grad_in(it, carry):
        rows = pl.ds(pl.multiple_of(it * 32, 32), 32)
        for g in range(GROUPS):
            gin_ref[rows, lanes(g)] = (
                gn_ref[0, 1, rows, lanes(g)].astype(F32) + z_ref[g, rows, :]
            ).astype(BF16)
        return carry

    lax.fori_loop(0, PIX // 32, to_grad_in, 0)
    result_copies[0].start()
    reduce_last(1)
    reduce_second(0)
    small_3(0)
    small_4(1)
    small_4(0)
    small_5(1)
    reduce_last(0)
    small_5(0)
    small_6(1)
    reduce_end(1)
    small_6(0)
    for copy in result_copies[1:5]:
        copy.start()
    reduce_end(0)
    for copy in result_copies[5:]:
        copy.start()

    for e in range(4):
        for n, d in enumerate(DIRS):

            @pl.when(exists(d))
            def _(e=e, n=n):
                halo_copy(e, n).wait_send()

    for l in range(2):
        for q in range(4):
            pair_copy(l, q).wait_send()
        for k in range(2):
            relay_copy(l, k).wait_send()
            first_copy(l, k).wait_send()
        for k in range(1, 4):
            second_copy(l, k).wait_send()
            small_first(l, k).wait_send()
            small_second(l, k).wait_send()
            small_gather(l, k).wait_send()
        for k in range(1, 8):
            small_z(l, k).wait_send()
        for q in range(16):

            @pl.when(jnp.logical_not(is_me(last_target(q))))
            def _(l=l, q=q):
                last_copy(l, q).wait_send()

        small_pair(l).wait_send()
        small_back(l).wait_send()
    for copy in result_copies:
        copy.wait()


def hand_over(*refs):
    srcs, dsts, mids, sem = refs[:7], refs[7:14], refs[14:21], refs[21]
    ins = [pltpu.make_async_copy(u, v, sem.at[n]) for n, (u, v) in enumerate(zip(srcs, mids))]
    outs = [pltpu.make_async_copy(u, v, sem.at[7 + n]) for n, (u, v) in enumerate(zip(mids, dsts))]
    for copy in ins:
        copy.start()
    for copy, then in zip(ins, outs):
        copy.wait()
        then.start()
    for copy in outs:
        copy.wait()


def shards(activations, grad_out, kernels, norm_gains, norm_shifts, w_in, b_in, w_out):
    hbm = pl.BlockSpec(memory_space=pl.ANY)
    dma = pltpu.SemaphoreType.DMA
    pad_size = PROWS * PITCH
    scratch = [
        pltpu.VMEM((PIX, C), BF16),
        pltpu.VMEM((7, 7, 2, C), F32),
        pltpu.VMEM((2, C), F32),
        pltpu.VMEM((2, C), F32),
        pltpu.VMEM((2, HID), F32),
        pltpu.VMEM((6, 2, C), F32),
        pltpu.VMEM((6, 2, C), F32),
        pltpu.VMEM((2, C), F32),
        pltpu.VMEM((2, C), F32),
        pltpu.VMEM((2, HID), F32),
        pltpu.VMEM((PIX, C), BF16),
        pltpu.VMEM((7, 7, 2, C), F32),
        pltpu.VMEM((2, C, HID), BF16),
        pltpu.VMEM((2, C, HID), BF16),
        pltpu.VMEM((4, GROUPS, pad_size, 128), F32),
        pltpu.VMEM((GROUPS, PIX, 128), F32),
        pltpu.VMEM((2, GROUPS, PIX, 128), F32),
        pltpu.VMEM((2, PIX, 128), F32),
        pltpu.VMEM((2, 2, PIX, HID), BF16),
        pltpu.VMEM((2, 2, PIX, C), BF16),
        pltpu.VMEM((2, PIX, HID), F32),
        pltpu.VMEM((PIX, HID), F32),
        pltpu.VMEM((2, PIX, CHUNK), F32),
        pltpu.VMEM((PIX, C), F32),
        pltpu.VMEM((2, HID), F32),
        pltpu.VMEM((4, 8, 48, C), BF16),
        pltpu.VMEM((4, 8, 48, C), BF16),
        pltpu.VMEM((2, 4, C, C), BF16),
        pltpu.VMEM((2, 4, C, C), BF16),
        pltpu.VMEM((2, C, C), BF16),
        pltpu.VMEM((2, 2, C // 2, C), BF16),
        pltpu.VMEM((2, 2, C, C), BF16),
        pltpu.VMEM((2, 2, C, C), BF16),
        pltpu.VMEM((2, 3, C, C), F32),
        pltpu.VMEM((2, 3, 96, C), BF16),
        pltpu.VMEM((2, 3, 96, C), BF16),
        pltpu.VMEM((96, C), F32),
        pltpu.VMEM((2, 16, 8, C), BF16),
        pltpu.VMEM((2, 16, 8, C), BF16),
        pltpu.VMEM((2, SMALL, C), F32),
        pltpu.VMEM((2, 32, C), F32),
        pltpu.VMEM((2, 4, 8, C), F32),
        pltpu.VMEM((2, 3, 8, C), F32),
        pltpu.VMEM((2, 4, 8, C), BF16),
        pltpu.VMEM((2, 8, 8, C), BF16),
        pltpu.VMEM((2, 4, 8, C), F32),
        pltpu.VMEM((2, 4, 8, C), F32),
        dma((17,)),
        dma((4, 8)),
        dma((4, 8)),
        dma((2, 4)),
        dma((2, 4)),
        dma((2, 2)),
        dma((2, 2)),
        dma((2, 2)),
        dma((2, 2)),
        dma((2, 3)),
        dma((2, 3)),
        dma((2, 16)),
        dma((2, 16)),
        dma((2,)),
        dma((2,)),
        dma((2, 3)),
        dma((2, 3)),
        dma((2, 3)),
        dma((2, 3)),
        dma((2, 7)),
        dma((2, 7)),
        dma((2, 3)),
        dma((2, 3)),
        dma((2,)),
        dma((2,)),
    ]
    sds = jax.ShapeDtypeStruct
    outs = pl.pallas_call(
        kernel,
        out_shape=(
            sds((PIX, C), BF16),
            sds((7, 7, 2, C), F32),
            sds((2, C), F32),
            sds((2, C), F32),
            sds((2, HID), F32),
            sds((6, 2, C), F32),
            sds((6, 2, C), F32),
        ),
        in_specs=[hbm] * 8,
        out_specs=(hbm,) * 7,
        scratch_shapes=scratch,
        compiler_params=pltpu.CompilerParams(
            collective_id=0, has_side_effects=True, vmem_limit_bytes=64000000
        ),
        name="convnext_step",
    )(
        activations.reshape(PIX, C),
        grad_out.reshape(PIX, C),
        jnp.transpose(kernels, (1, 2, 0, 3)),
        norm_gains,
        norm_shifts,
        w_in,
        b_in,
        w_out,
    )
    grad_in, gk, gg, gs, gb, gwi, gwo = pl.pallas_call(
        hand_over,
        out_shape=tuple(sds(o.shape, o.dtype) for o in outs),
        in_specs=[hbm] * 7,
        out_specs=(hbm,) * 7,
        scratch_shapes=[pltpu.VMEM(o.shape, o.dtype) for o in outs] + [dma((14,))],
        name="hand_over",
    )(*outs)
    return (
        grad_in.reshape(activations.shape),
        jnp.transpose(gk, (2, 0, 1, 3)),
        gg,
        gs,
        gb,
        jnp.transpose(gwi, (1, 2, 0)),
        jnp.transpose(gwo, (1, 2, 0)),
    )


def solution(mesh):
    return jax.shard_map(
        shards,
        mesh=mesh,
        in_specs=(P("rows", "cols", None), P("rows", "cols", None), P(), P(), P(), P(), P(), P()),
        out_specs=(
            P("rows", "cols", None),
            P(),
            P(),
            P(),
            P(),
            P(None, None, ("rows", "cols")),
            P(None, None, ("rows", "cols")),
        ),
        check_vma=False,
    )
```

```python
import functools
import math

import jax
import jax.numpy as jnp
from jax import lax
from jax.experimental import pallas as pl
from jax.experimental.pallas import tpu as pltpu
from jax.sharding import PartitionSpec as P

EPSILON = 1e-06
ROOT_HALF = 0.7071067811865476
INV_ROOT_TAU = 0.3989422804014327
MESH = pl.DeviceIdType.MESH
F32 = jnp.float32
BF16 = jnp.bfloat16

C = 384
HID = 1536
TILE = 16
PIX = TILE * TILE
PITCH = 32
PROWS = TILE + 6
GROUPS = C // 128
CHUNK = 256
SMALL = 64
DIRS = tuple((dr, dc) for dr in (-1, 0, 1) for dc in (-1, 0, 1) if (dr, dc) != (0, 0))
TN = (((0,), (0,)), ((), ()))
NT = (((1,), (1,)), ((), ()))


def lanes(g):
    return pl.ds(g * 128, 128)


def gelu_parts(pre):
    cdf = 0.5 * (1.0 + lax.erf(pre * ROOT_HALF))
    density = jnp.exp(-0.5 * pre * pre) * INV_ROOT_TAU
    return pre * cdf, cdf + pre * density


def pad_row(i):
    return (i + 3) * PITCH + 8


def conv_into(src, kern, layer, flip, emit):
    block = 4

    def step(it, carry):
        g = it // (TILE // block)
        row = (it % (TILE // block)) * block
        col = pl.ds(pl.multiple_of(g * 128, 128), 128)
        acc = [[None, None] for _ in range(block)]
        for rho in range(block + 6):
            taps = [
                src[g, pl.ds((row + rho) * PITCH + 5 + s, 8, stride=2), :] for s in range(8)
            ]
            for i in range(block):
                a = rho - i
                if a < 0 or a > 6:
                    continue
                for b in range(7):
                    ka, kb = (6 - a, 6 - b) if flip else (a, b)
                    w = kern[ka, kb, pl.ds(layer, 1), col]
                    for par in range(2):
                        term = taps[b + par] * w
                        acc[i][par] = term if acc[i][par] is None else acc[i][par] + term
        for i in range(block):
            for par in range(2):
                emit(g, row + i, par, acc[i][par])
        return carry

    lax.fori_loop(0, GROUPS * (TILE // block), step, 0)


def conv_sides(src, kern, layer, out):
    def step(g, carry):
        col = pl.ds(pl.multiple_of(g * 128, 128), 128)
        for side in range(2):
            acc = {}
            for q in range(3):
                at = 5 + q if side == 0 else 24 + q
                for a in range(7):
                    for half in range(2):
                        v = src[g, pl.ds((a + 8 * half) * PITCH + at, 8, stride=PITCH), :]
                        for j in range(3):
                            b = q - j if side == 0 else 6 + q - j
                            if b < 0 or b > 6:
                                continue
                            term = v * kern[a, b, pl.ds(layer, 1), col]
                            key = (j, half)
                            acc[key] = term if key not in acc else acc[key] + term
            for (j, half), value in acc.items():
                own = j if side == 0 else 13 + j
                at = pl.ds(8 * half * TILE + own, 8, stride=TILE)
                out[g, at, :] = out[g, at, :] + value
        return carry

    lax.fori_loop(0, GROUPS, step, 0)


def conv_ends(src, kern, layer, out):
    def step(g, carry):
        col = pl.ds(pl.multiple_of(g * 128, 128), 128)
        for rhos in (range(0, 3), range(19, 22)):
            acc = {}
            for rho in rhos:
                taps = [src[g, pl.ds(rho * PITCH + 5 + s, 8, stride=2), :] for s in range(8)]
                for a in range(7):
                    i = rho - a
                    if i < 0 or i >= TILE:
                        continue
                    for b in range(7):
                        w = kern[a, b, pl.ds(layer, 1), col]
                        for par in range(2):
                            term = taps[b + par] * w
                            key = (i, par)
                            acc[key] = term if key not in acc else acc[key] + term
            for (i, par), value in acc.items():
                at = pl.ds(i * TILE + par, 8, stride=2)
                out[g, at, :] = out[g, at, :] + value
        return carry

    lax.fori_loop(0, GROUPS, step, 0)


def taps_grad(grad, src, small, layer):
    def step(it, carry):
        g = it // 7
        a = it % 7
        col = pl.ds(pl.multiple_of(g * 128, 128), 128)
        acc = [None] * 7
        for i in range(TILE):
            dz = [grad[g, pl.ds(pad_row(i) + par, 8, stride=2), :] for par in range(2)]
            row = [src[g, pl.ds((i + a) * PITCH + 5 + s, 8, stride=2), :] for s in range(8)]
            for b in range(7):
                term = dz[0] * row[b] + dz[1] * row[b + 1]
                acc[b] = term if acc[b] is None else acc[b] + term
        rows = [jnp.sum(acc[b], axis=0, keepdims=True) for b in range(7)]
        rows.append(jnp.zeros((1, 128), F32))
        small[layer, pl.ds(pl.multiple_of(a * 8, 8), 8), col] = jnp.concatenate(rows, axis=0)
        return carry

    lax.fori_loop(0, GROUPS * 7, step, 0)


def kernel(
    act_hbm,
    gout_hbm,
    kern_hbm,
    gain_hbm,
    shift_hbm,
    win_hbm,
    bin_hbm,
    wout_hbm,
    gin_hbm,
    gk_hbm,
    gg_hbm,
    gs_hbm,
    gb_hbm,
    gwi_hbm,
    gwo_hbm,
    gin_ref,
    gk_ref,
    gg_ref,
    gs_ref,
    gb_ref,
    gwi_ref,
    gwo_ref,
    gain_ref,
    shift_ref,
    bin_ref,
    act_ref,
    kern_ref,
    win,
    wout,
    pads,
    z_ref,
    hat_ref,
    inv_ref,
    hid_ref,
    gn_ref,
    slope_ref,
    ga_ref,
    pre_ref,
    dn_ref,
    db_ref,
    hsend,
    hrecv,
    csend,
    crecv,
    s0,
    r0,
    s1,
    r1,
    own1,
    s2,
    r2,
    own2,
    s3,
    r3,
    small,
    smc,
    smt,
    sma,
    smb,
    smz,
    smg,
    smx,
    wsem,
    hs,
    hr,
    cs,
    cr,
    p0s,
    p0r,
    p1s,
    p1r,
    p2s,
    p2r,
    p3s,
    p3r,
    mcs,
    mcr,
    mas,
    mar,
    mbs,
    mbr,
    mzs,
    mzr,
    mgs,
    mgr,
    mxs,
    mxr,
):
    r = lax.axis_index("rows")
    c = lax.axis_index("cols")
    y, zl = r // 4, r % 4
    x, zh, core = c // 4, (c // 2) % 2, c % 2
    z = zh * 4 + zl
    first = y * (1 - core) + x * core
    second = x * (1 - core) + y * core
    scale = 1.0 / math.sqrt(256 * 256)

    def device(dx, dy, dz, dcore):
        return (dy * 4 + dz % 4, dx * 4 + (dz // 4) * 2 + dcore)

    def first_peer(k):
        q = (first + k) % 4
        return device(x * (1 - core) + q * core, q * (1 - core) + y * core, z, core)

    def second_peer(k):
        q = (second + k) % 4
        return device(q * (1 - core) + x * core, y * (1 - core) + q * core, z, core)

    def z_peer(k):
        return device(x, y, (z + k) % 8, core)

    def last_target(q):
        return device(q // 4, first, (q // 2 % 2) * 4 + second, q % 2)

    def last_source(q):
        return device(zl, y, q, 0) if q < 8 else device(y, zl, q - 8, 1)

    partner = (r, c + 1 - 2 * core)

    def is_me(dev):
        return jnp.logical_and(dev[0] == r, dev[1] == c)

    def exists(d):
        rr, cc = r + d[0], c + d[1]
        return jnp.logical_and(
            jnp.logical_and(rr >= 0, rr < 16), jnp.logical_and(cc >= 0, cc < 16)
        )

    act_copy = pltpu.make_async_copy(act_hbm, act_ref, wsem.at[4])
    act_copy.start()
    kern_copy = pltpu.make_async_copy(kern_hbm, kern_ref, wsem.at[5])
    gout_copy = pltpu.make_async_copy(gout_hbm, gn_ref.at[1, 1], wsem.at[6])
    kern_copy.start()
    gout_copy.start()
    vector_copies = [
        pltpu.make_async_copy(src, dst, wsem.at[7 + n])
        for n, (src, dst) in enumerate(
            ((gain_hbm, gain_ref), (shift_hbm, shift_ref), (bin_hbm, bin_ref))
        )
    ]
    for copy in vector_copies:
        copy.start()
    result_copies = [
        pltpu.make_async_copy(src, dst, wsem.at[10 + n])
        for n, (src, dst) in enumerate(
            (
                (gin_ref, gin_hbm),
                (gk_ref, gk_hbm),
                (gg_ref, gg_hbm),
                (gs_ref, gs_hbm),
                (gb_ref, gb_hbm),
                (gwi_ref, gwi_hbm),
                (gwo_ref, gwo_hbm),
            )
        )
    ]

    barrier = pltpu.get_barrier_semaphore()

    def greet(dev):
        pl.semaphore_signal(barrier, inc=1, device_id=dev, device_id_type=MESH)

    count = jnp.int32(13)
    for d in DIRS:
        ok = exists(d)

        @pl.when(ok)
        def _(d=d):
            greet((r + d[0], c + d[1]))

        count = count + ok.astype(jnp.int32)
    for k in range(1, 4):
        greet(first_peer(k))
        greet(second_peer(k))
    for k in range(1, 8):
        greet(z_peer(k))
    for q in range(16):
        for dev in (last_target(q), last_source(q)):
            away = jnp.logical_not(is_me(dev))

            @pl.when(away)
            def _(dev=dev):
                greet(dev)

            count = count + away.astype(jnp.int32)

    weight_copies = []
    for n, (src, dst, l) in enumerate(
        ((win_hbm, win, 0), (wout_hbm, wout, 0), (win_hbm, win, 1), (wout_hbm, wout, 1))
    ):
        copy = pltpu.make_async_copy(src.at[l], dst.at[l], wsem.at[n])
        copy.start()
        weight_copies.append(copy)

    zero = jnp.zeros((PITCH, 128), F32)

    def clear(it, carry):
        for p in range(4):
            for g in range(GROUPS):
                pads[p, g, pl.ds(pl.multiple_of(it * PITCH, PITCH), PITCH), :] = zero
        return carry

    lax.fori_loop(0, PROWS, clear, 0)
    act_copy.wait()

    def fill(it, carry):
        rows = pl.ds(pl.multiple_of(it * TILE, TILE), TILE)
        for g in range(GROUPS):
            pads[0, g, pl.ds(pl.multiple_of(pad_row(it), 8), TILE), :] = act_ref[
                rows, lanes(g)
            ].astype(F32)
        return carry

    lax.fori_loop(0, TILE, fill, 0)

    def halo_copy(e, n):
        d = DIRS[n]
        size = 16 if d[0] != 0 and d[1] != 0 else 48
        return pltpu.make_async_remote_copy(
            src_ref=hsend.at[e, n, pl.ds(0, size)],
            dst_ref=hrecv.at[e, 7 - n, pl.ds(0, size)],
            send_sem=hs.at[n],
            recv_sem=hr.at[e % 2, 7 - n],
            device_id=(r + d[0], c + d[1]),
            device_id_type=MESH,
        )

    def halo_start(e, p):
        for n, d in enumerate(DIRS):
            row0 = {-1: 0, 0: 0, 1: TILE - 3}[d[0]]
            for g in range(GROUPS):
                if d[1] == 0:
                    for k in range(3):
                        hsend[e, n, pl.ds(k * 16, 16), lanes(g)] = pads[
                            p, g, pl.ds(pad_row(row0 + k), TILE), :
                        ].astype(BF16)
                elif d[0] == 0:
                    col0 = 0 if d[1] < 0 else TILE - 3
                    for k in range(3):
                        hsend[e, n, pl.ds(k * 16, 16), lanes(g)] = pads[
                            p, g, pl.ds(pad_row(0) + col0 + k, TILE, stride=PITCH), :
                        ].astype(BF16)
                else:
                    col0 = 0 if d[1] < 0 else 8
                    cut = slice(0, 3) if d[1] < 0 else slice(5, 8)
                    parts = [
                        pads[p, g, pl.ds(pad_row(row0 + k) + col0, 8), :] for k in range(3)
                    ]
                    hsend[e, n, pl.ds(0, 16), lanes(g)] = jnp.concatenate(
                        [v[cut] for v in parts] + [parts[0][0:7]], axis=0
                    ).astype(BF16)

            @pl.when(exists(d))
            def _(n=n):
                halo_copy(e, n).start()

    def halo_finish(e, p, sides=(True, False)):
        for n, d in enumerate(DIRS):
            if (d[0] == 0) not in sides:
                continue

            @pl.when(exists(d))
            def _(n=n, d=d):
                size = 16 if d[0] != 0 and d[1] != 0 else 48
                pltpu.make_async_remote_copy(
                    src_ref=hsend.at[e, n, pl.ds(0, size)],
                    dst_ref=hrecv.at[e, n, pl.ds(0, size)],
                    send_sem=hs.at[n],
                    recv_sem=hr.at[e % 2, n],
                    device_id=(r + d[0], c + d[1]),
                    device_id_type=MESH,
                ).wait_recv()
                row0 = {-1: -3, 0: 0, 1: TILE}[d[0]]
                for g in range(GROUPS):
                    got = hrecv[e, n, pl.ds(0, size), lanes(g)].astype(F32)
                    if d[1] == 0:
                        for k in range(3):
                            pads[p, g, pl.ds(pad_row(row0 + k), TILE), :] = got[
                                k * 16 : k * 16 + 16
                            ]
                    elif d[0] == 0:
                        col0 = -3 if d[1] < 0 else TILE
                        for k in range(3):
                            pads[
                                p, g, pl.ds(pad_row(0) + col0 + k, TILE, stride=PITCH), :
                            ] = got[k * 16 : k * 16 + 16]
                    else:
                        col0 = -3 if d[1] < 0 else TILE
                        for k in range(3):
                            pads[p, g, pl.ds(pad_row(row0 + k) + col0, 3), :] = got[
                                k * 3 : k * 3 + 3
                            ]

    pl.semaphore_wait(barrier, count)
    halo_start(0, 0)
    kern_copy.wait()
    for copy in vector_copies:
        copy.wait()

    def forward_conv(layer, p):
        def emit(g, i, par, value):
            z_ref[g, pl.ds(i * TILE + par, 8, stride=2), :] = value

        conv_into(pads.at[p], kern_ref, layer, False, emit)

    def halo_conv(layer, e, p):
        halo_finish(e, p, (True,))
        conv_sides(pads.at[p], kern_ref, layer, z_ref)
        halo_finish(e, p, (False,))
        conv_ends(pads.at[p], kern_ref, layer, z_ref)

    def forward_norm(layer, p):
        def step(it, carry):
            rows = pl.ds(pl.multiple_of(it * 32, 32), 32)
            zs = [z_ref[g, rows, :] for g in range(GROUPS)]
            mean = jnp.sum(zs[0] + zs[1] + zs[2], axis=-1, keepdims=True) * (1.0 / C)
            cen = [v - mean for v in zs]
            var = jnp.sum(
                cen[0] * cen[0] + cen[1] * cen[1] + cen[2] * cen[2], axis=-1, keepdims=True
            ) * (1.0 / C)
            inv = lax.rsqrt(var + EPSILON)
            inv_ref[layer, rows, :] = jnp.broadcast_to(inv, (32, 128))
            for g in range(GROUPS):
                hat = cen[g] * inv
                hat_ref[layer, g, rows, :] = hat
                gn_ref[layer, 0, rows, lanes(g)] = (
                    hat * gain_ref[pl.ds(layer, 1), lanes(g)]
                    + shift_ref[pl.ds(layer, 1), lanes(g)]
                ).astype(BF16)
            return carry

        lax.fori_loop(0, PIX // 32, step, 0, unroll=4)

    def hidden_forward(layer):
        steps = HID // CHUNK

        def product(n):
            pre_ref[n % 2] = jnp.dot(
                gn_ref[layer, 0], win[layer, :, n * CHUNK : (n + 1) * CHUNK], preferred_element_type=F32
            )

        product(0)
        for n in range(steps):
            cols = pl.ds(n * CHUNK, CHUNK)
            if n + 1 < steps:
                product(n + 1)
            bias = bin_ref[pl.ds(layer, 1), cols]
            for it in range(PIX // 32):
                rows = pl.ds(it * 32, 32)
                act, slope = gelu_parts(pre_ref[n % 2, rows, :] + bias)
                hid_ref[layer, 1, rows, cols] = act.astype(BF16)
                slope_ref[layer, rows, cols] = slope

    def hidden_grad(layer):
        for n in range(HID // CHUNK):
            cols = pl.ds(n * CHUNK, CHUNK)
            ga_ref[:, cols] = jnp.dot(
                gn_ref[layer, 1], wout[layer, :, cols], preferred_element_type=F32
            )

    def slope_times(layer, matmul):
        steps = HID // CHUNK

        def product(n):
            cols = pl.ds(n * CHUNK, CHUNK)
            ga_ref[:, cols] = jnp.dot(
                gn_ref[layer, 1], wout[layer, :, cols], preferred_element_type=F32
            )

        if matmul:
            product(0)
        for n in range(steps):
            cols = pl.ds(n * CHUNK, CHUNK)
            if matmul and n + 1 < steps:
                product(n + 1)
            total = jnp.zeros((8, CHUNK), F32)
            for it in range(PIX // 32):
                rows = pl.ds(it * 32, 32)
                grad = ga_ref[rows, cols] * slope_ref[layer, rows, cols]
                hid_ref[layer, 0, rows, cols] = grad.astype(BF16)
                total = total + (grad[0:8] + grad[8:16]) + (grad[16:24] + grad[24:32])
            db_ref[pl.ds(layer, 1), cols] = jnp.sum(total, axis=0, keepdims=True)

    def norm_grad(layer, p):
        dn_ref[...] = lax.dot_general(
            hid_ref[layer, 0], win[layer], NT, preferred_element_type=F32
        )

        def step(it, carry):
            carry = list(carry)
            rows = pl.ds(pl.multiple_of(it * 32, 32), 32)
            dn = [dn_ref[rows, lanes(g)] for g in range(GROUPS)]
            hat = [hat_ref[layer, g, rows, :] for g in range(GROUPS)]
            sc = [dn[g] * gain_ref[pl.ds(layer, 1), lanes(g)] for g in range(GROUPS)]
            m1 = jnp.sum(sc[0] + sc[1] + sc[2], axis=-1, keepdims=True) * (1.0 / C)
            m2 = jnp.sum(
                sc[0] * hat[0] + sc[1] * hat[1] + sc[2] * hat[2], axis=-1, keepdims=True
            ) * (1.0 / C)
            inv = inv_ref[layer, rows, :]
            for g in range(GROUPS):
                dz = (inv * (sc[g] - m1 - hat[g] * m2)).astype(BF16).astype(F32)
                for k in range(2):
                    pads[
                        p, g, pl.ds(pl.multiple_of(pad_row(it * 2 + k), 8), TILE), :
                    ] = dz[k * TILE : (k + 1) * TILE]
                prod = dn[g] * hat[g]
                carry[g] += (prod[0:8] + prod[8:16]) + (prod[16:24] + prod[24:32])
                carry[3 + g] += (dn[g][0:8] + dn[g][8:16]) + (dn[g][16:24] + dn[g][24:32])
            return tuple(carry)

        sums = lax.fori_loop(
            0, PIX // 32, step, (jnp.zeros((8, 128), F32),) * 6, unroll=4
        )
        for g in range(GROUPS):
            for k in range(2):
                small[layer, pl.ds(56 + k, 1), lanes(g)] = jnp.sum(
                    sums[3 * k + g], axis=0, keepdims=True
                )
        for k in range(4):
            small[layer, pl.ds(58 + k, 1), :] = db_ref[pl.ds(layer, 1), pl.ds(k * C, C)]
        small[layer, pl.ds(62, 2), :] = jnp.zeros((2, C), F32)

    def remote(src, dst, ssem, rsem, dev):
        return pltpu.make_async_remote_copy(
            src_ref=src,
            dst_ref=dst,
            send_sem=ssem,
            recv_sem=rsem,
            device_id=dev,
            device_id_type=MESH,
        )

    def pair_copy(l, q):
        return remote(csend.at[l, q], crecv.at[l, q], cs.at[l], cr.at[l, q], partner)

    def relay_copy(l, k):
        return remote(
            s0.at[l, pl.ds(192 * k, 192)], r0.at[l, k], p0s.at[l], p0r.at[l, k], first_peer(1 + 2 * k)
        )

    def first_copy(l, k):
        return remote(s1.at[l, k], r1.at[l, k], p1s.at[l], p1r.at[l], first_peer(1 + 2 * k))

    def second_copy(l, k):
        return remote(
            s2.at[l, k - 1], r2.at[l, k - 1], p2s.at[l], p2r.at[l], second_peer(k)
        )

    def last_copy(l, q):
        slot = core * 8 + z
        return remote(s3.at[l, q], r3.at[l, slot], p3s.at[l], p3r.at[l], last_target(q))

    def first_all(l):
        return remote(s1.at[l], r1.at[l], p1s.at[l], p1r.at[l], partner)

    def second_all(l):
        return remote(s2.at[l], r2.at[l], p2s.at[l], p2r.at[l], partner)

    def last_all(l, n):
        part = pl.ds(0, n)
        return remote(s3.at[l, part], r3.at[l, part], p3s.at[l], p3r.at[l], partner)

    keeps = jnp.logical_and(first == y, second == zl)

    def weight_grad(l, m, q):
        return lax.dot_general(
            hid_ref[l, m, :, pl.ds(pl.multiple_of(q * C, C), C)],
            gn_ref[l, m],
            TN,
            preferred_element_type=F32,
        )

    def reduce_start(l):
        for k in (2, 3, 1, 0):
            q = (second + k) % 4
            csend[l, q] = weight_grad(l, 1 - core, q).astype(BF16)
            pair_copy(l, q).start()

    def pair_block(l, k):
        q = (first + k) % 4
        mine = weight_grad(l, core, q)
        pair_copy(l, q).wait_recv()
        return mine + crecv[l, q].astype(F32)

    def reduce_relay(l):
        s0[l] = pair_block(l, 2).astype(BF16)
        for k in range(2):
            relay_copy(l, k).start()

    def reduce_pair(l):
        for i, k in enumerate((3, 1, 0)):
            own1[l, i] = pair_block(l, k)

    def reduce_first(l):
        for k in range(2):
            relay_copy(l, k).wait_recv()
            part = pl.ds(192 * k, 192)
            rest = pl.ds(192 * (1 - k), 192)
            s1[l, k, part, :] = (own1[l, 1 - k, part, :] + r0[l, k].astype(F32)).astype(BF16)
            s1[l, k, rest, :] = own1[l, 1 - k, rest, :].astype(BF16)
            first_copy(l, k).start()

    def reduce_second(l):
        first_all(l).wait_recv()

        def block(k):
            rows = pl.ds(pl.multiple_of(((second + k) % 4) * 96, 96), 96)
            return (
                own1[l, 2, rows, :]
                + r1[l, 0, rows, :].astype(F32)
                + r1[l, 1, rows, :].astype(F32)
            )

        def step(k, carry):
            s2[l, k - 1] = block(k).astype(BF16)
            second_copy(l, k).start()
            return carry

        lax.fori_loop(1, 4, step, 0)
        own2[...] = block(0)

    def reduce_last(l):
        second_all(l).wait_recv()
        total = (
            own2[...]
            + r2[l, 0].astype(F32)
            + r2[l, 1].astype(F32)
            + r2[l, 2].astype(F32)
        )
        for q in range(16):
            piece = total[6 * q : 6 * q + 6]
            s3[l, q] = jnp.concatenate([piece, piece[0:2]], axis=0).astype(BF16)
            me = is_me(last_target(q))

            @pl.when(jnp.logical_not(me))
            def _(q=q):
                last_copy(l, q).start()

            @pl.when(me)
            def _(q=q):
                r3[l, core * 8 + z] = s3[l, q]

    def reduce_end(l):
        @pl.when(jnp.logical_not(keeps))
        def _():
            last_all(l, 16).wait_recv()

        @pl.when(keeps)
        def _():
            last_all(l, 15).wait_recv()

        for m, out in ((0, gwi_ref), (1, gwo_ref)):
            total = r3[l, 8 * m].astype(F32)
            for q in range(1, 8):
                total = total + r3[l, 8 * m + q].astype(F32)
            total = total * scale
            for j in range(6):
                out[j, pl.ds(l, 1), :] = total[j : j + 1]

    def small_pair(l):
        half = pl.ds(pl.multiple_of((1 - core) * 32, 32), 32)
        return remote(small.at[l, half], smc.at[l], mcs.at[l], mcr.at[l], partner)

    def small_first(l, k):
        q = (first + k) % 4
        return remote(
            smt.at[l, q], sma.at[l, k - 1], mas.at[l], mar.at[l], first_peer(k)
        )

    def small_second(l, k):
        return remote(
            smb.at[l, second],
            smb.at[l, second],
            mbs.at[l],
            mbr.at[l],
            second_peer(k),
        )

    def small_z(l, k):
        return remote(
            smz.at[l, z], smz.at[l, z], mzs.at[l], mzr.at[l], z_peer(k)
        )

    def small_gather(l, k):
        return remote(
            smg.at[l, first], smg.at[l, first], mgs.at[l], mgr.at[l], first_peer(k)
        )

    def small_back(l):
        return remote(smg.at[l], smx.at[l], mxs.at[l], mxr.at[l], partner)

    def small_first_all(l):
        return remote(smt.at[l, pl.ds(0, 3)], sma.at[l], mas.at[l], mar.at[l], partner)

    def small_second_all(l):
        part = smb.at[l, pl.ds(0, 3)]
        return remote(part, part, mbs.at[l], mbr.at[l], partner)

    def small_z_all(l):
        part = smz.at[l, pl.ds(0, 7)]
        return remote(part, part, mzs.at[l], mzr.at[l], partner)

    def small_gather_all(l):
        part = smg.at[l, pl.ds(0, 3)]
        return remote(part, part, mgs.at[l], mgr.at[l], partner)

    def small_0(l):
        small_pair(l).start()

    def small_1(l):
        small_pair(l).wait_recv()
        for q in range(4):
            rows = pl.ds(pl.multiple_of(core * 32 + q * 8, 8), 8)
            smt[l, q] = small[l, rows, :] + smc[l, pl.ds(q * 8, 8), :]
        for k in range(1, 4):
            small_first(l, k).start()

    def small_2(l):
        small_first_all(l).wait_recv()
        total = (smt[l, first] + sma[l, 0]) + (sma[l, 1] + sma[l, 2])
        smb[l, second] = total.astype(BF16)
        for k in range(1, 4):
            small_second(l, k).start()

    def small_3(l):
        small_second_all(l).wait_recv()
        part = [smb[l, q].astype(F32) for q in range(4)]
        smz[l, z] = ((part[0] + part[1]) + (part[2] + part[3])).astype(BF16)
        for k in range(1, 8):
            small_z(l, k).start()

    def small_4(l):
        small_z_all(l).wait_recv()
        total = smz[l, 0].astype(F32)
        for q in range(1, 8):
            total = total + smz[l, q].astype(F32)
        smg[l, first] = total * scale
        for k in range(1, 4):
            small_gather(l, k).start()

    def small_5(l):
        small_gather_all(l).wait_recv()
        small_back(l).start()

    def small_6(l):
        small_back(l).wait_recv()
        zeroth = core == 0
        low = [jnp.where(zeroth, smg[l, q], smx[l, q]) for q in range(4)]
        high = [jnp.where(zeroth, smx[l, q], smg[l, q]) for q in range(4)]
        full = jnp.concatenate(low + high, axis=0)
        for a in range(7):
            for b in range(7):
                gk_ref[a, b, pl.ds(l, 1), :] = full[a * 8 + b : a * 8 + b + 1]
        gg_ref[pl.ds(l, 1), :] = full[56:57]
        gs_ref[pl.ds(l, 1), :] = full[57:58]
        for k in range(4):
            gb_ref[pl.ds(l, 1), pl.ds(k * C, C)] = full[58 + k : 59 + k]

    forward_conv(0, 0)
    halo_conv(0, 0, 0)
    forward_norm(0, 0)
    for copy in weight_copies:
        copy.wait()
    hidden_forward(0)
    dn_ref[...] = lax.dot_general(hid_ref[0, 1], wout[0], NT, preferred_element_type=F32)

    def to_middle(it, carry):
        rows = pl.ds(pl.multiple_of(it * TILE, TILE), TILE)
        at = pl.ds(pl.multiple_of(pad_row(it), 8), TILE)
        for g in range(GROUPS):
            pads[1, g, at, :] = (pads[0, g, at, :] + dn_ref[rows, lanes(g)]).astype(BF16).astype(F32)
        return carry

    lax.fori_loop(0, TILE, to_middle, 0)
    halo_start(1, 1)
    gout_copy.wait()
    hidden_grad(1)
    forward_conv(1, 1)
    halo_conv(1, 1, 1)
    forward_norm(1, 1)
    hidden_forward(1)
    slope_times(1, False)
    norm_grad(1, 2)
    halo_start(2, 2)
    taps_grad(pads.at[2], pads.at[1], small, 1)
    small_0(1)
    reduce_start(1)
    reduce_relay(1)
    small_1(1)
    reduce_pair(1)
    halo_finish(2, 2)

    def emit_mid(g, i, par, value):
        z_ref[g, pl.ds(i * TILE + par, 8, stride=2), :] = value

    conv_into(pads.at[2], kern_ref, 1, True, emit_mid)

    def to_grad_mid(it, carry):
        rows = pl.ds(pl.multiple_of(it * 32, 32), 32)
        for g in range(GROUPS):
            gn_ref[0, 1, rows, lanes(g)] = (
                gn_ref[1, 1, rows, lanes(g)].astype(F32) + z_ref[g, rows, :]
            ).astype(BF16)
        return carry

    lax.fori_loop(0, PIX // 32, to_grad_mid, 0)
    slope_times(0, True)
    reduce_first(1)
    reduce_start(0)
    norm_grad(0, 3)
    halo_start(3, 3)
    reduce_relay(0)
    taps_grad(pads.at[3], pads.at[0], small, 0)
    small_0(0)
    small_2(1)
    reduce_pair(0)
    small_1(0)
    reduce_first(0)
    reduce_second(1)
    small_3(1)
    halo_finish(3, 3)
    small_2(0)
    conv_into(pads.at[3], kern_ref, 0, True, emit_mid)

    def to_grad_in(it, carry):
        rows = pl.ds(pl.multiple_of(it * 32, 32), 32)
        for g in range(GROUPS):
            gin_ref[rows, lanes(g)] = (
                gn_ref[0, 1, rows, lanes(g)].astype(F32) + z_ref[g, rows, :]
            ).astype(BF16)
        return carry

    lax.fori_loop(0, PIX // 32, to_grad_in, 0)
    result_copies[0].start()
    reduce_last(1)
    reduce_second(0)
    small_3(0)
    small_4(1)
    small_4(0)
    small_5(1)
    reduce_last(0)
    small_5(0)
    small_6(1)
    reduce_end(1)
    small_6(0)
    for copy in result_copies[1:5]:
        copy.start()
    reduce_end(0)
    for copy in result_copies[5:]:
        copy.start()

    for n, d in enumerate(DIRS):

        @pl.when(exists(d))
        def _(n=n, d=d):
            size = 16 if d[0] != 0 and d[1] != 0 else 48
            part = hsend.at[pl.ds(0, 4), n, pl.ds(0, size)]
            remote(part, part, hs.at[n], hr.at[0, n], partner).wait_send()

    for l in range(2):
        remote(csend.at[l], crecv.at[l], cs.at[l], cr.at[l, 0], partner).wait_send()
        remote(s0.at[l], s0.at[l], p0s.at[l], p0r.at[l, 0], partner).wait_send()
        first_all(l).wait_send()
        second_all(l).wait_send()
        small_first_all(l).wait_send()
        small_second_all(l).wait_send()
        small_z_all(l).wait_send()
        small_gather_all(l).wait_send()

        @pl.when(jnp.logical_not(keeps))
        def _(l=l):
            last_all(l, 16).wait_send()

        @pl.when(keeps)
        def _(l=l):
            last_all(l, 15).wait_send()

        small_pair(l).wait_send()
        small_back(l).wait_send()
    for copy in result_copies:
        copy.wait()


def hand_over(*refs):
    srcs, dsts, mids, sem = refs[:7], refs[7:14], refs[14:21], refs[21]
    ins = [pltpu.make_async_copy(u, v, sem.at[n]) for n, (u, v) in enumerate(zip(srcs, mids))]
    outs = [pltpu.make_async_copy(u, v, sem.at[7 + n]) for n, (u, v) in enumerate(zip(mids, dsts))]
    for copy in ins:
        copy.start()
    for copy, then in zip(ins, outs):
        copy.wait()
        then.start()
    for copy in outs:
        copy.wait()


def shards(activations, grad_out, kernels, norm_gains, norm_shifts, w_in, b_in, w_out):
    hbm = pl.BlockSpec(memory_space=pl.ANY)
    dma = pltpu.SemaphoreType.DMA
    pad_size = PROWS * PITCH
    scratch = [
        pltpu.VMEM((PIX, C), BF16),
        pltpu.VMEM((7, 7, 2, C), F32),
        pltpu.VMEM((2, C), F32),
        pltpu.VMEM((2, C), F32),
        pltpu.VMEM((2, HID), F32),
        pltpu.VMEM((6, 2, C), F32),
        pltpu.VMEM((6, 2, C), F32),
        pltpu.VMEM((2, C), F32),
        pltpu.VMEM((2, C), F32),
        pltpu.VMEM((2, HID), F32),
        pltpu.VMEM((PIX, C), BF16),
        pltpu.VMEM((7, 7, 2, C), F32),
        pltpu.VMEM((2, C, HID), BF16),
        pltpu.VMEM((2, C, HID), BF16),
        pltpu.VMEM((4, GROUPS, pad_size, 128), F32),
        pltpu.VMEM((GROUPS, PIX, 128), F32),
        pltpu.VMEM((2, GROUPS, PIX, 128), F32),
        pltpu.VMEM((2, PIX, 128), F32),
        pltpu.VMEM((2, 2, PIX, HID), BF16),
        pltpu.VMEM((2, 2, PIX, C), BF16),
        pltpu.VMEM((2, PIX, HID), F32),
        pltpu.VMEM((PIX, HID), F32),
        pltpu.VMEM((2, PIX, CHUNK), F32),
        pltpu.VMEM((PIX, C), F32),
        pltpu.VMEM((2, HID), F32),
        pltpu.VMEM((4, 8, 48, C), BF16),
        pltpu.VMEM((4, 8, 48, C), BF16),
        pltpu.VMEM((2, 4, C, C), BF16),
        pltpu.VMEM((2, 4, C, C), BF16),
        pltpu.VMEM((2, C, C), BF16),
        pltpu.VMEM((2, 2, C // 2, C), BF16),
        pltpu.VMEM((2, 2, C, C), BF16),
        pltpu.VMEM((2, 2, C, C), BF16),
        pltpu.VMEM((2, 3, C, C), F32),
        pltpu.VMEM((2, 3, 96, C), BF16),
        pltpu.VMEM((2, 3, 96, C), BF16),
        pltpu.VMEM((96, C), F32),
        pltpu.VMEM((2, 16, 8, C), BF16),
        pltpu.VMEM((2, 16, 8, C), BF16),
        pltpu.VMEM((2, SMALL, C), F32),
        pltpu.VMEM((2, 32, C), F32),
        pltpu.VMEM((2, 4, 8, C), F32),
        pltpu.VMEM((2, 3, 8, C), F32),
        pltpu.VMEM((2, 4, 8, C), BF16),
        pltpu.VMEM((2, 8, 8, C), BF16),
        pltpu.VMEM((2, 4, 8, C), F32),
        pltpu.VMEM((2, 4, 8, C), F32),
        dma((17,)),
        dma((8,)),
        dma((2, 8)),
        dma((2,)),
        dma((2, 4)),
        dma((2,)),
        dma((2, 2)),
    ] + [dma((2,))] * 18
    sds = jax.ShapeDtypeStruct
    outs = pl.pallas_call(
        kernel,
        out_shape=(
            sds((PIX, C), BF16),
            sds((7, 7, 2, C), F32),
            sds((2, C), F32),
            sds((2, C), F32),
            sds((2, HID), F32),
            sds((6, 2, C), F32),
            sds((6, 2, C), F32),
        ),
        in_specs=[hbm] * 8,
        out_specs=(hbm,) * 7,
        scratch_shapes=scratch,
        compiler_params=pltpu.CompilerParams(
            collective_id=0, has_side_effects=True, vmem_limit_bytes=64000000
        ),
        name="convnext_step",
    )(
        activations.reshape(PIX, C),
        grad_out.reshape(PIX, C),
        jnp.transpose(kernels, (1, 2, 0, 3)),
        norm_gains,
        norm_shifts,
        w_in,
        b_in,
        w_out,
    )
    grad_in, gk, gg, gs, gb, gwi, gwo = pl.pallas_call(
        hand_over,
        out_shape=tuple(sds(o.shape, o.dtype) for o in outs),
        in_specs=[hbm] * 7,
        out_specs=(hbm,) * 7,
        scratch_shapes=[pltpu.VMEM(o.shape, o.dtype) for o in outs] + [dma((14,))],
        name="hand_over",
    )(*outs)
    return (
        grad_in.reshape(activations.shape),
        jnp.transpose(gk, (2, 0, 1, 3)),
        gg,
        gs,
        gb,
        jnp.transpose(gwi, (1, 2, 0)),
        jnp.transpose(gwo, (1, 2, 0)),
    )


def solution(mesh):
    return jax.shard_map(
        shards,
        mesh=mesh,
        in_specs=(P("rows", "cols", None), P("rows", "cols", None), P(), P(), P(), P(), P(), P()),
        out_specs=(
            P("rows", "cols", None),
            P(),
            P(),
            P(),
            P(),
            P(None, None, ("rows", "cols")),
            P(None, None, ("rows", "cols")),
        ),
        check_vma=False,
    )
```

```python
import functools
import math

import jax
import jax.numpy as jnp
from jax import lax
from jax.experimental import pallas as pl
from jax.experimental.pallas import tpu as pltpu
from jax.sharding import PartitionSpec as P

EPSILON = 1e-06
ROOT_HALF = 0.7071067811865476
INV_ROOT_TAU = 0.3989422804014327
MESH = pl.DeviceIdType.MESH
F32 = jnp.float32
BF16 = jnp.bfloat16

C = 384
HID = 1536
TILE = 16
PIX = TILE * TILE
PITCH = 32
PROWS = TILE + 6
GROUPS = C // 128
CHUNK = 256
SMALL = 64
DIRS = tuple((dr, dc) for dr in (-1, 0, 1) for dc in (-1, 0, 1) if (dr, dc) != (0, 0))
TN = (((0,), (0,)), ((), ()))
NT = (((1,), (1,)), ((), ()))


def lanes(g):
    return pl.ds(g * 128, 128)


def gelu_parts(pre):
    cdf = 0.5 * (1.0 + lax.erf(pre * ROOT_HALF))
    density = jnp.exp(-0.5 * pre * pre) * INV_ROOT_TAU
    return pre * cdf, cdf + pre * density


def pad_row(i):
    return (i + 3) * PITCH + 8


def conv_into(src, kern, layer, flip, emit):
    block = 4

    def step(it, carry):
        g = it // (TILE // block)
        row = (it % (TILE // block)) * block
        col = pl.ds(pl.multiple_of(g * 128, 128), 128)
        acc = [[None, None] for _ in range(block)]
        for rho in range(block + 6):
            taps = [
                src[g, pl.ds((row + rho) * PITCH + 5 + s, 8, stride=2), :] for s in range(8)
            ]
            for i in range(block):
                a = rho - i
                if a < 0 or a > 6:
                    continue
                for b in range(7):
                    ka, kb = (6 - a, 6 - b) if flip else (a, b)
                    w = kern[ka, kb, pl.ds(layer, 1), col]
                    for par in range(2):
                        term = taps[b + par] * w
                        acc[i][par] = term if acc[i][par] is None else acc[i][par] + term
        for i in range(block):
            for par in range(2):
                emit(g, row + i, par, acc[i][par])
        return carry

    lax.fori_loop(0, GROUPS * (TILE // block), step, 0)


def conv_sides(src, kern, layer, out):
    def step(g, carry):
        col = pl.ds(pl.multiple_of(g * 128, 128), 128)
        for side in range(2):
            acc = {}
            for q in range(3):
                at = 5 + q if side == 0 else 24 + q
                for a in range(7):
                    for half in range(2):
                        v = src[g, pl.ds((a + 8 * half) * PITCH + at, 8, stride=PITCH), :]
                        for j in range(3):
                            b = q - j if side == 0 else 6 + q - j
                            if b < 0 or b > 6:
                                continue
                            term = v * kern[a, b, pl.ds(layer, 1), col]
                            key = (j, half)
                            acc[key] = term if key not in acc else acc[key] + term
            for (j, half), value in acc.items():
                own = j if side == 0 else 13 + j
                at = pl.ds(8 * half * TILE + own, 8, stride=TILE)
                out[g, at, :] = out[g, at, :] + value
        return carry

    lax.fori_loop(0, GROUPS, step, 0)


def conv_ends(src, kern, layer, out):
    def step(g, carry):
        col = pl.ds(pl.multiple_of(g * 128, 128), 128)
        for rhos in (range(0, 3), range(19, 22)):
            acc = {}
            for rho in rhos:
                taps = [src[g, pl.ds(rho * PITCH + 5 + s, 8, stride=2), :] for s in range(8)]
                for a in range(7):
                    i = rho - a
                    if i < 0 or i >= TILE:
                        continue
                    for b in range(7):
                        w = kern[a, b, pl.ds(layer, 1), col]
                        for par in range(2):
                            term = taps[b + par] * w
                            key = (i, par)
                            acc[key] = term if key not in acc else acc[key] + term
            for (i, par), value in acc.items():
                at = pl.ds(i * TILE + par, 8, stride=2)
                out[g, at, :] = out[g, at, :] + value
        return carry

    lax.fori_loop(0, GROUPS, step, 0)


def taps_grad(grad, src, small, layer):
    def step(it, carry):
        g = it // 7
        a = it % 7
        col = pl.ds(pl.multiple_of(g * 128, 128), 128)
        acc = [None] * 7
        for i in range(TILE):
            dz = [grad[g, pl.ds(pad_row(i) + par, 8, stride=2), :] for par in range(2)]
            row = [src[g, pl.ds((i + a) * PITCH + 5 + s, 8, stride=2), :] for s in range(8)]
            for b in range(7):
                term = dz[0] * row[b] + dz[1] * row[b + 1]
                acc[b] = term if acc[b] is None else acc[b] + term
        rows = [jnp.sum(acc[b], axis=0, keepdims=True) for b in range(7)]
        rows.append(jnp.zeros((1, 128), F32))
        small[layer, pl.ds(pl.multiple_of(a * 8, 8), 8), col] = jnp.concatenate(rows, axis=0)
        return carry

    lax.fori_loop(0, GROUPS * 7, step, 0)


def kernel(
    act_hbm,
    gout_hbm,
    kern_hbm,
    gain_hbm,
    shift_hbm,
    win_hbm,
    bin_hbm,
    wout_hbm,
    gin_hbm,
    gk_hbm,
    gg_hbm,
    gs_hbm,
    gb_hbm,
    gwi_hbm,
    gwo_hbm,
    gin_ref,
    gk_ref,
    gg_ref,
    gs_ref,
    gb_ref,
    gwi_ref,
    gwo_ref,
    gain_ref,
    shift_ref,
    bin_ref,
    act_ref,
    kern_ref,
    win,
    wout,
    pads,
    z_ref,
    hat_ref,
    inv_ref,
    hid_ref,
    gn_ref,
    slope_ref,
    ga_ref,
    pre_ref,
    dn_ref,
    db_ref,
    hsend,
    hrecv,
    csend,
    crecv,
    s0,
    r0,
    s1,
    r1,
    own1,
    s2,
    r2,
    own2,
    s3,
    r3,
    small,
    smc,
    smt,
    sma,
    smb,
    smz,
    smg,
    smx,
    wsem,
    hs,
    hr,
    cs,
    cr,
    p0s,
    p0r,
    p1s,
    p1r,
    p2s,
    p2r,
    p3s,
    p3r,
    mcs,
    mcr,
    mas,
    mar,
    mbs,
    mbr,
    mzs,
    mzr,
    mgs,
    mgr,
    mxs,
    mxr,
):
    r = lax.axis_index("rows")
    c = lax.axis_index("cols")
    y, zl = r // 4, r % 4
    x, zh, core = c // 4, (c // 2) % 2, c % 2
    z = zh * 4 + zl
    first = y * (1 - core) + x * core
    second = x * (1 - core) + y * core
    scale = 1.0 / math.sqrt(256 * 256)

    def device(dx, dy, dz, dcore):
        return (dy * 4 + dz % 4, dx * 4 + (dz // 4) * 2 + dcore)

    def first_peer(k):
        q = (first + k) % 4
        return device(x * (1 - core) + q * core, q * (1 - core) + y * core, z, core)

    def second_peer(k):
        q = (second + k) % 4
        return device(q * (1 - core) + x * core, y * (1 - core) + q * core, z, core)

    def z_peer(k):
        return device(x, y, (z + k) % 8, core)

    def last_target(q):
        return device(q // 4, first, (q // 2 % 2) * 4 + second, q % 2)

    def last_source(q):
        return device(zl, y, q, 0) if q < 8 else device(y, zl, q - 8, 1)

    partner = (r, c + 1 - 2 * core)

    def is_me(dev):
        return jnp.logical_and(dev[0] == r, dev[1] == c)

    def exists(d):
        rr, cc = r + d[0], c + d[1]
        return jnp.logical_and(
            jnp.logical_and(rr >= 0, rr < 16), jnp.logical_and(cc >= 0, cc < 16)
        )

    act_copy = pltpu.make_async_copy(act_hbm, act_ref, wsem.at[4])
    act_copy.start()
    kern_copy = pltpu.make_async_copy(kern_hbm, kern_ref, wsem.at[5])
    gout_copy = pltpu.make_async_copy(gout_hbm, gn_ref.at[1, 1], wsem.at[6])
    kern_copy.start()
    gout_copy.start()
    vector_copies = [
        pltpu.make_async_copy(src, dst, wsem.at[7 + n])
        for n, (src, dst) in enumerate(
            ((gain_hbm, gain_ref), (shift_hbm, shift_ref), (bin_hbm, bin_ref))
        )
    ]
    for copy in vector_copies:
        copy.start()
    result_copies = [
        pltpu.make_async_copy(src, dst, wsem.at[10 + n])
        for n, (src, dst) in enumerate(
            (
                (gin_ref, gin_hbm),
                (gk_ref, gk_hbm),
                (gg_ref, gg_hbm),
                (gs_ref, gs_hbm),
                (gb_ref, gb_hbm),
                (gwi_ref, gwi_hbm),
                (gwo_ref, gwo_hbm),
            )
        )
    ]

    barrier = pltpu.get_barrier_semaphore()

    def greet(dev):
        pl.semaphore_signal(barrier, inc=1, device_id=dev, device_id_type=MESH)

    count = jnp.int32(13)
    for d in DIRS:
        ok = exists(d)

        @pl.when(ok)
        def _(d=d):
            greet((r + d[0], c + d[1]))

        count = count + ok.astype(jnp.int32)
    for k in range(1, 4):
        greet(first_peer(k))
        greet(second_peer(k))
    for k in range(1, 8):
        greet(z_peer(k))
    for q in range(16):
        for dev in (last_target(q), last_source(q)):
            away = jnp.logical_not(is_me(dev))

            @pl.when(away)
            def _(dev=dev):
                greet(dev)

            count = count + away.astype(jnp.int32)

    weight_copies = []
    for n, (src, dst, l) in enumerate(
        ((win_hbm, win, 0), (wout_hbm, wout, 0), (win_hbm, win, 1), (wout_hbm, wout, 1))
    ):
        copy = pltpu.make_async_copy(src.at[l], dst.at[l], wsem.at[n])
        copy.start()
        weight_copies.append(copy)

    zero = jnp.zeros((PITCH, 128), F32)

    def clear(it, carry):
        for p in range(4):
            for g in range(GROUPS):
                pads[p, g, pl.ds(pl.multiple_of(it * PITCH, PITCH), PITCH), :] = zero
        return carry

    lax.fori_loop(0, PROWS, clear, 0)
    act_copy.wait()

    def fill(it, carry):
        rows = pl.ds(pl.multiple_of(it * TILE, TILE), TILE)
        for g in range(GROUPS):
            pads[0, g, pl.ds(pl.multiple_of(pad_row(it), 8), TILE), :] = act_ref[
                rows, lanes(g)
            ].astype(F32)
        return carry

    lax.fori_loop(0, TILE, fill, 0)

    def halo_copy(e, n):
        d = DIRS[n]
        size = 16 if d[0] != 0 and d[1] != 0 else 48
        return pltpu.make_async_remote_copy(
            src_ref=hsend.at[e, n, pl.ds(0, size)],
            dst_ref=hrecv.at[e, 7 - n, pl.ds(0, size)],
            send_sem=hs.at[n],
            recv_sem=hr.at[e % 2, 7 - n],
            device_id=(r + d[0], c + d[1]),
            device_id_type=MESH,
        )

    def halo_start(e, p):
        for n, d in enumerate(DIRS):
            row0 = {-1: 0, 0: 0, 1: TILE - 3}[d[0]]
            for g in range(GROUPS):
                if d[1] == 0:
                    for k in range(3):
                        hsend[e, n, pl.ds(k * 16, 16), lanes(g)] = pads[
                            p, g, pl.ds(pad_row(row0 + k), TILE), :
                        ].astype(BF16)
                elif d[0] == 0:
                    col0 = 0 if d[1] < 0 else TILE - 3
                    for k in range(3):
                        hsend[e, n, pl.ds(k * 16, 16), lanes(g)] = pads[
                            p, g, pl.ds(pad_row(0) + col0 + k, TILE, stride=PITCH), :
                        ].astype(BF16)
                else:
                    col0 = 0 if d[1] < 0 else 8
                    cut = slice(0, 3) if d[1] < 0 else slice(5, 8)
                    parts = [
                        pads[p, g, pl.ds(pad_row(row0 + k) + col0, 8), :] for k in range(3)
                    ]
                    hsend[e, n, pl.ds(0, 16), lanes(g)] = jnp.concatenate(
                        [v[cut] for v in parts] + [parts[0][0:7]], axis=0
                    ).astype(BF16)

            @pl.when(exists(d))
            def _(n=n):
                halo_copy(e, n).start()

    def halo_finish(e, p, sides=(True, False)):
        for n, d in enumerate(DIRS):
            if (d[0] == 0) not in sides:
                continue

            @pl.when(exists(d))
            def _(n=n, d=d):
                size = 16 if d[0] != 0 and d[1] != 0 else 48
                pltpu.make_async_remote_copy(
                    src_ref=hsend.at[e, n, pl.ds(0, size)],
                    dst_ref=hrecv.at[e, n, pl.ds(0, size)],
                    send_sem=hs.at[n],
                    recv_sem=hr.at[e % 2, n],
                    device_id=(r + d[0], c + d[1]),
                    device_id_type=MESH,
                ).wait_recv()
                row0 = {-1: -3, 0: 0, 1: TILE}[d[0]]
                for g in range(GROUPS):
                    got = hrecv[e, n, pl.ds(0, size), lanes(g)].astype(F32)
                    if d[1] == 0:
                        for k in range(3):
                            pads[p, g, pl.ds(pad_row(row0 + k), TILE), :] = got[
                                k * 16 : k * 16 + 16
                            ]
                    elif d[0] == 0:
                        col0 = -3 if d[1] < 0 else TILE
                        for k in range(3):
                            pads[
                                p, g, pl.ds(pad_row(0) + col0 + k, TILE, stride=PITCH), :
                            ] = got[k * 16 : k * 16 + 16]
                    else:
                        col0 = -3 if d[1] < 0 else TILE
                        for k in range(3):
                            pads[p, g, pl.ds(pad_row(row0 + k) + col0, 3), :] = got[
                                k * 3 : k * 3 + 3
                            ]

    pl.semaphore_wait(barrier, count)
    halo_start(0, 0)
    kern_copy.wait()
    for copy in vector_copies:
        copy.wait()

    def forward_conv(layer, p):
        def emit(g, i, par, value):
            z_ref[g, pl.ds(i * TILE + par, 8, stride=2), :] = value

        conv_into(pads.at[p], kern_ref, layer, False, emit)

    def halo_conv(layer, e, p):
        halo_finish(e, p, (True,))
        conv_sides(pads.at[p], kern_ref, layer, z_ref)
        halo_finish(e, p, (False,))
        conv_ends(pads.at[p], kern_ref, layer, z_ref)

    def forward_norm(layer, p):
        def step(it, carry):
            rows = pl.ds(pl.multiple_of(it * 32, 32), 32)
            zs = [z_ref[g, rows, :] for g in range(GROUPS)]
            mean = jnp.sum(zs[0] + zs[1] + zs[2], axis=-1, keepdims=True) * (1.0 / C)
            cen = [v - mean for v in zs]
            var = jnp.sum(
                cen[0] * cen[0] + cen[1] * cen[1] + cen[2] * cen[2], axis=-1, keepdims=True
            ) * (1.0 / C)
            inv = lax.rsqrt(var + EPSILON)
            inv_ref[layer, rows, :] = jnp.broadcast_to(inv, (32, 128))
            for g in range(GROUPS):
                hat = cen[g] * inv
                hat_ref[layer, g, rows, :] = hat
                gn_ref[layer, 0, rows, lanes(g)] = (
                    hat * gain_ref[pl.ds(layer, 1), lanes(g)]
                    + shift_ref[pl.ds(layer, 1), lanes(g)]
                ).astype(BF16)
            return carry

        lax.fori_loop(0, PIX // 32, step, 0, unroll=4)

    def hidden_forward(layer):
        steps = HID // CHUNK

        def product(n):
            pre_ref[n % 2] = jnp.dot(
                gn_ref[layer, 0], win[layer, :, n * CHUNK : (n + 1) * CHUNK], preferred_element_type=F32
            )

        product(0)
        for n in range(steps):
            cols = pl.ds(n * CHUNK, CHUNK)
            if n + 1 < steps:
                product(n + 1)
            bias = bin_ref[pl.ds(layer, 1), cols]
            for it in range(PIX // 32):
                rows = pl.ds(it * 32, 32)
                act, slope = gelu_parts(pre_ref[n % 2, rows, :] + bias)
                hid_ref[layer, 1, rows, cols] = act.astype(BF16)
                slope_ref[layer, rows, cols] = slope

    def hidden_grad(layer):
        for n in range(HID // CHUNK):
            cols = pl.ds(n * CHUNK, CHUNK)
            ga_ref[:, cols] = jnp.dot(
                gn_ref[layer, 1], wout[layer, :, cols], preferred_element_type=F32
            )

    def slope_times(layer, matmul):
        steps = HID // CHUNK

        def product(n):
            cols = pl.ds(n * CHUNK, CHUNK)
            ga_ref[:, cols] = jnp.dot(
                gn_ref[layer, 1], wout[layer, :, cols], preferred_element_type=F32
            )

        if matmul:
            product(0)
        for n in range(steps):
            cols = pl.ds(n * CHUNK, CHUNK)
            if matmul and n + 1 < steps:
                product(n + 1)
            total = jnp.zeros((8, CHUNK), F32)
            for it in range(PIX // 32):
                rows = pl.ds(it * 32, 32)
                grad = ga_ref[rows, cols] * slope_ref[layer, rows, cols]
                hid_ref[layer, 0, rows, cols] = grad.astype(BF16)
                total = total + (grad[0:8] + grad[8:16]) + (grad[16:24] + grad[24:32])
            db_ref[pl.ds(layer, 1), cols] = jnp.sum(total, axis=0, keepdims=True)

    def norm_grad(layer, p):
        dn_ref[...] = lax.dot_general(
            hid_ref[layer, 0], win[layer], NT, preferred_element_type=F32
        )

        def step(it, carry):
            carry = list(carry)
            rows = pl.ds(pl.multiple_of(it * 32, 32), 32)
            dn = [dn_ref[rows, lanes(g)] for g in range(GROUPS)]
            hat = [hat_ref[layer, g, rows, :] for g in range(GROUPS)]
            sc = [dn[g] * gain_ref[pl.ds(layer, 1), lanes(g)] for g in range(GROUPS)]
            m1 = jnp.sum(sc[0] + sc[1] + sc[2], axis=-1, keepdims=True) * (1.0 / C)
            m2 = jnp.sum(
                sc[0] * hat[0] + sc[1] * hat[1] + sc[2] * hat[2], axis=-1, keepdims=True
            ) * (1.0 / C)
            inv = inv_ref[layer, rows, :]
            for g in range(GROUPS):
                dz = (inv * (sc[g] - m1 - hat[g] * m2)).astype(BF16).astype(F32)
                for k in range(2):
                    pads[
                        p, g, pl.ds(pl.multiple_of(pad_row(it * 2 + k), 8), TILE), :
                    ] = dz[k * TILE : (k + 1) * TILE]
                prod = dn[g] * hat[g]
                carry[g] += (prod[0:8] + prod[8:16]) + (prod[16:24] + prod[24:32])
                carry[3 + g] += (dn[g][0:8] + dn[g][8:16]) + (dn[g][16:24] + dn[g][24:32])
            return tuple(carry)

        sums = lax.fori_loop(
            0, PIX // 32, step, (jnp.zeros((8, 128), F32),) * 6, unroll=4
        )
        for g in range(GROUPS):
            for k in range(2):
                small[layer, pl.ds(56 + k, 1), lanes(g)] = jnp.sum(
                    sums[3 * k + g], axis=0, keepdims=True
                )
        for k in range(4):
            small[layer, pl.ds(58 + k, 1), :] = db_ref[pl.ds(layer, 1), pl.ds(k * C, C)]
        small[layer, pl.ds(62, 2), :] = jnp.zeros((2, C), F32)

    def remote(src, dst, ssem, rsem, dev):
        return pltpu.make_async_remote_copy(
            src_ref=src,
            dst_ref=dst,
            send_sem=ssem,
            recv_sem=rsem,
            device_id=dev,
            device_id_type=MESH,
        )

    def pair_copy(l, q):
        return remote(csend.at[l, q], crecv.at[l, q], cs.at[l], cr.at[l, q], partner)

    def relay_copy(l, k):
        return remote(
            s0.at[l, pl.ds(192 * k, 192)], r0.at[l, k], p0s.at[l], p0r.at[l, k], first_peer(1 + 2 * k)
        )

    def first_copy(l, k):
        return remote(s1.at[l, k], r1.at[l, k], p1s.at[l], p1r.at[l], first_peer(1 + 2 * k))

    def second_copy(l, k):
        return remote(
            s2.at[l, k - 1], r2.at[l, k - 1], p2s.at[l], p2r.at[l], second_peer(k)
        )

    def last_copy(l, q):
        slot = core * 8 + z
        return remote(s3.at[l, q], r3.at[l, slot], p3s.at[l], p3r.at[l], last_target(q))

    def first_all(l):
        return remote(s1.at[l], r1.at[l], p1s.at[l], p1r.at[l], partner)

    def second_all(l):
        return remote(s2.at[l], r2.at[l], p2s.at[l], p2r.at[l], partner)

    def last_all(l, n):
        part = pl.ds(0, n)
        return remote(s3.at[l, part], r3.at[l, part], p3s.at[l], p3r.at[l], partner)

    keeps = jnp.logical_and(first == y, second == zl)

    def weight_grad(l, m, q):
        return lax.dot_general(
            hid_ref[l, m, :, pl.ds(pl.multiple_of(q * C, C), C)],
            gn_ref[l, m],
            TN,
            preferred_element_type=F32,
        )

    def reduce_start(l):
        for k in (2, 3, 1, 0):
            q = (second + k) % 4
            csend[l, q] = weight_grad(l, 1 - core, q).astype(BF16)
            pair_copy(l, q).start()

    def pair_block(l, k):
        q = (first + k) % 4
        mine = weight_grad(l, core, q)
        pair_copy(l, q).wait_recv()
        return mine + crecv[l, q].astype(F32)

    def reduce_relay(l):
        s0[l] = pair_block(l, 2).astype(BF16)
        for k in range(2):
            relay_copy(l, k).start()

    def reduce_pair(l):
        for i, k in enumerate((3, 1, 0)):
            own1[l, i] = pair_block(l, k)

    def reduce_first(l):
        for k in range(2):
            relay_copy(l, k).wait_recv()
            part = pl.ds(192 * k, 192)
            rest = pl.ds(192 * (1 - k), 192)
            s1[l, k, part, :] = (own1[l, 1 - k, part, :] + r0[l, k].astype(F32)).astype(BF16)
            s1[l, k, rest, :] = own1[l, 1 - k, rest, :].astype(BF16)
            first_copy(l, k).start()

    def reduce_second(l):
        first_all(l).wait_recv()

        def block(k):
            rows = pl.ds(pl.multiple_of(((second + k) % 4) * 96, 96), 96)
            return (
                own1[l, 2, rows, :]
                + r1[l, 0, rows, :].astype(F32)
                + r1[l, 1, rows, :].astype(F32)
            )

        def step(k, carry):
            s2[l, k - 1] = block(k).astype(BF16)
            second_copy(l, k).start()
            return carry

        lax.fori_loop(1, 4, step, 0)
        own2[...] = block(0)

    def reduce_last(l):
        second_all(l).wait_recv()
        total = (
            own2[...]
            + r2[l, 0].astype(F32)
            + r2[l, 1].astype(F32)
            + r2[l, 2].astype(F32)
        )
        for q in range(16):
            piece = total[6 * q : 6 * q + 6]
            s3[l, q] = jnp.concatenate([piece, piece[0:2]], axis=0).astype(BF16)
            me = is_me(last_target(q))

            @pl.when(jnp.logical_not(me))
            def _(q=q):
                last_copy(l, q).start()

            @pl.when(me)
            def _(q=q):
                r3[l, core * 8 + z] = s3[l, q]

    def reduce_end(l):
        @pl.when(jnp.logical_not(keeps))
        def _():
            last_all(l, 16).wait_recv()

        @pl.when(keeps)
        def _():
            last_all(l, 15).wait_recv()

        for m, out in ((0, gwi_ref), (1, gwo_ref)):
            total = r3[l, 8 * m].astype(F32)
            for q in range(1, 8):
                total = total + r3[l, 8 * m + q].astype(F32)
            total = total * scale
            for j in range(6):
                out[j, pl.ds(l, 1), :] = total[j : j + 1]

    def small_pair(l):
        half = pl.ds(pl.multiple_of((1 - core) * 32, 32), 32)
        return remote(small.at[l, half], smc.at[l], mcs.at[l], mcr.at[l], partner)

    def small_first(l, k):
        q = (first + k) % 4
        return remote(
            smt.at[l, q], sma.at[l, k - 1], mas.at[l], mar.at[l], first_peer(k)
        )

    def small_second(l, k):
        return remote(
            smb.at[l, second],
            smb.at[l, second],
            mbs.at[l],
            mbr.at[l],
            second_peer(k),
        )

    def small_z(l, k):
        return remote(
            smz.at[l, z], smz.at[l, z], mzs.at[l], mzr.at[l], z_peer(k)
        )

    def small_gather(l, k):
        return remote(
            smg.at[l, first], smg.at[l, first], mgs.at[l], mgr.at[l], first_peer(k)
        )

    def small_back(l):
        return remote(smg.at[l], smx.at[l], mxs.at[l], mxr.at[l], partner)

    def small_first_all(l):
        return remote(smt.at[l, pl.ds(0, 3)], sma.at[l], mas.at[l], mar.at[l], partner)

    def small_second_all(l):
        part = smb.at[l, pl.ds(0, 3)]
        return remote(part, part, mbs.at[l], mbr.at[l], partner)

    def small_z_all(l):
        part = smz.at[l, pl.ds(0, 7)]
        return remote(part, part, mzs.at[l], mzr.at[l], partner)

    def small_gather_all(l):
        part = smg.at[l, pl.ds(0, 3)]
        return remote(part, part, mgs.at[l], mgr.at[l], partner)

    def small_0(l):
        small_pair(l).start()

    def small_1(l):
        small_pair(l).wait_recv()
        for q in range(4):
            rows = pl.ds(pl.multiple_of(core * 32 + q * 8, 8), 8)
            smt[l, q] = small[l, rows, :] + smc[l, pl.ds(q * 8, 8), :]
        for k in range(1, 4):
            small_first(l, k).start()

    def small_2(l):
        small_first_all(l).wait_recv()
        total = (smt[l, first] + sma[l, 0]) + (sma[l, 1] + sma[l, 2])
        smb[l, second] = total.astype(BF16)
        for k in range(1, 4):
            small_second(l, k).start()

    def small_3(l):
        small_second_all(l).wait_recv()
        part = [smb[l, q].astype(F32) for q in range(4)]
        smz[l, z] = ((part[0] + part[1]) + (part[2] + part[3])).astype(BF16)
        for k in range(1, 8):
            small_z(l, k).start()

    def small_4(l):
        small_z_all(l).wait_recv()
        total = smz[l, 0].astype(F32)
        for q in range(1, 8):
            total = total + smz[l, q].astype(F32)
        smg[l, first] = total * scale
        for k in range(1, 4):
            small_gather(l, k).start()

    def small_5(l):
        small_gather_all(l).wait_recv()
        small_back(l).start()

    def small_6(l):
        small_back(l).wait_recv()
        zeroth = core == 0
        low = [jnp.where(zeroth, smg[l, q], smx[l, q]) for q in range(4)]
        high = [jnp.where(zeroth, smx[l, q], smg[l, q]) for q in range(4)]
        full = jnp.concatenate(low + high, axis=0)
        for a in range(7):
            for b in range(7):
                gk_ref[a, b, pl.ds(l, 1), :] = full[a * 8 + b : a * 8 + b + 1]
        gg_ref[pl.ds(l, 1), :] = full[56:57]
        gs_ref[pl.ds(l, 1), :] = full[57:58]
        for k in range(4):
            gb_ref[pl.ds(l, 1), pl.ds(k * C, C)] = full[58 + k : 59 + k]

    forward_conv(0, 0)
    halo_conv(0, 0, 0)
    forward_norm(0, 0)
    for copy in weight_copies:
        copy.wait()
    hidden_forward(0)
    dn_ref[...] = lax.dot_general(hid_ref[0, 1], wout[0], NT, preferred_element_type=F32)

    def to_middle(it, carry):
        rows = pl.ds(pl.multiple_of(it * TILE, TILE), TILE)
        at = pl.ds(pl.multiple_of(pad_row(it), 8), TILE)
        for g in range(GROUPS):
            pads[1, g, at, :] = (pads[0, g, at, :] + dn_ref[rows, lanes(g)]).astype(BF16).astype(F32)
        return carry

    lax.fori_loop(0, TILE, to_middle, 0)
    halo_start(1, 1)
    gout_copy.wait()
    hidden_grad(1)
    forward_conv(1, 1)
    halo_conv(1, 1, 1)
    forward_norm(1, 1)
    hidden_forward(1)
    slope_times(1, False)
    norm_grad(1, 2)
    halo_start(2, 2)
    taps_grad(pads.at[2], pads.at[1], small, 1)
    small_0(1)
    reduce_start(1)
    reduce_relay(1)
    small_1(1)
    reduce_pair(1)
    halo_finish(2, 2)

    def emit_mid(g, i, par, value):
        z_ref[g, pl.ds(i * TILE + par, 8, stride=2), :] = value

    conv_into(pads.at[2], kern_ref, 1, True, emit_mid)

    def to_grad_mid(it, carry):
        rows = pl.ds(pl.multiple_of(it * 32, 32), 32)
        for g in range(GROUPS):
            gn_ref[0, 1, rows, lanes(g)] = (
                gn_ref[1, 1, rows, lanes(g)].astype(F32) + z_ref[g, rows, :]
            ).astype(BF16)
        return carry

    lax.fori_loop(0, PIX // 32, to_grad_mid, 0)
    reduce_first(1)
    slope_times(0, True)
    reduce_start(0)
    norm_grad(0, 3)
    halo_start(3, 3)
    reduce_relay(0)
    taps_grad(pads.at[3], pads.at[0], small, 0)
    small_0(0)
    small_2(1)
    reduce_pair(0)
    small_1(0)
    reduce_first(0)
    reduce_second(1)
    small_3(1)
    halo_finish(3, 3)
    small_2(0)
    conv_into(pads.at[3], kern_ref, 0, True, emit_mid)

    def to_grad_in(it, carry):
        rows = pl.ds(pl.multiple_of(it * 32, 32), 32)
        for g in range(GROUPS):
            gin_ref[rows, lanes(g)] = (
                gn_ref[0, 1, rows, lanes(g)].astype(F32) + z_ref[g, rows, :]
            ).astype(BF16)
        return carry

    lax.fori_loop(0, PIX // 32, to_grad_in, 0)
    result_copies[0].start()
    reduce_last(1)
    reduce_second(0)
    small_3(0)
    small_4(1)
    small_4(0)
    small_5(1)
    reduce_last(0)
    small_5(0)
    small_6(1)
    reduce_end(1)
    small_6(0)
    for copy in result_copies[1:5]:
        copy.start()
    reduce_end(0)
    for copy in result_copies[5:]:
        copy.start()

    for n, d in enumerate(DIRS):

        @pl.when(exists(d))
        def _(n=n, d=d):
            size = 16 if d[0] != 0 and d[1] != 0 else 48
            part = hsend.at[pl.ds(0, 4), n, pl.ds(0, size)]
            remote(part, part, hs.at[n], hr.at[0, n], partner).wait_send()

    for l in range(2):
        remote(csend.at[l], crecv.at[l], cs.at[l], cr.at[l, 0], partner).wait_send()
        remote(s0.at[l], s0.at[l], p0s.at[l], p0r.at[l, 0], partner).wait_send()
        first_all(l).wait_send()
        second_all(l).wait_send()
        small_first_all(l).wait_send()
        small_second_all(l).wait_send()
        small_z_all(l).wait_send()
        small_gather_all(l).wait_send()

        @pl.when(jnp.logical_not(keeps))
        def _(l=l):
            last_all(l, 16).wait_send()

        @pl.when(keeps)
        def _(l=l):
            last_all(l, 15).wait_send()

        small_pair(l).wait_send()
        small_back(l).wait_send()
    for copy in result_copies:
        copy.wait()


def hand_over(*refs):
    srcs, dsts, mids, sem = refs[:7], refs[7:14], refs[14:21], refs[21]
    ins = [pltpu.make_async_copy(u, v, sem.at[n]) for n, (u, v) in enumerate(zip(srcs, mids))]
    outs = [pltpu.make_async_copy(u, v, sem.at[7 + n]) for n, (u, v) in enumerate(zip(mids, dsts))]
    for copy in ins:
        copy.start()
    for copy, then in zip(ins, outs):
        copy.wait()
        then.start()
    for copy in outs:
        copy.wait()


def shards(activations, grad_out, kernels, norm_gains, norm_shifts, w_in, b_in, w_out):
    hbm = pl.BlockSpec(memory_space=pl.ANY)
    dma = pltpu.SemaphoreType.DMA
    pad_size = PROWS * PITCH
    scratch = [
        pltpu.VMEM((PIX, C), BF16),
        pltpu.VMEM((7, 7, 2, C), F32),
        pltpu.VMEM((2, C), F32),
        pltpu.VMEM((2, C), F32),
        pltpu.VMEM((2, HID), F32),
        pltpu.VMEM((6, 2, C), F32),
        pltpu.VMEM((6, 2, C), F32),
        pltpu.VMEM((2, C), F32),
        pltpu.VMEM((2, C), F32),
        pltpu.VMEM((2, HID), F32),
        pltpu.VMEM((PIX, C), BF16),
        pltpu.VMEM((7, 7, 2, C), F32),
        pltpu.VMEM((2, C, HID), BF16),
        pltpu.VMEM((2, C, HID), BF16),
        pltpu.VMEM((4, GROUPS, pad_size, 128), F32),
        pltpu.VMEM((GROUPS, PIX, 128), F32),
        pltpu.VMEM((2, GROUPS, PIX, 128), F32),
        pltpu.VMEM((2, PIX, 128), F32),
        pltpu.VMEM((2, 2, PIX, HID), BF16),
        pltpu.VMEM((2, 2, PIX, C), BF16),
        pltpu.VMEM((2, PIX, HID), F32),
        pltpu.VMEM((PIX, HID), F32),
        pltpu.VMEM((2, PIX, CHUNK), F32),
        pltpu.VMEM((PIX, C), F32),
        pltpu.VMEM((2, HID), F32),
        pltpu.VMEM((4, 8, 48, C), BF16),
        pltpu.VMEM((4, 8, 48, C), BF16),
        pltpu.VMEM((2, 4, C, C), BF16),
        pltpu.VMEM((2, 4, C, C), BF16),
        pltpu.VMEM((2, C, C), BF16),
        pltpu.VMEM((2, 2, C // 2, C), BF16),
        pltpu.VMEM((2, 2, C, C), BF16),
        pltpu.VMEM((2, 2, C, C), BF16),
        pltpu.VMEM((2, 3, C, C), F32),
        pltpu.VMEM((2, 3, 96, C), BF16),
        pltpu.VMEM((2, 3, 96, C), BF16),
        pltpu.VMEM((96, C), F32),
        pltpu.VMEM((2, 16, 8, C), BF16),
        pltpu.VMEM((2, 16, 8, C), BF16),
        pltpu.VMEM((2, SMALL, C), F32),
        pltpu.VMEM((2, 32, C), F32),
        pltpu.VMEM((2, 4, 8, C), F32),
        pltpu.VMEM((2, 3, 8, C), F32),
        pltpu.VMEM((2, 4, 8, C), BF16),
        pltpu.VMEM((2, 8, 8, C), BF16),
        pltpu.VMEM((2, 4, 8, C), F32),
        pltpu.VMEM((2, 4, 8, C), F32),
        dma((17,)),
        dma((8,)),
        dma((2, 8)),
        dma((2,)),
        dma((2, 4)),
        dma((2,)),
        dma((2, 2)),
    ] + [dma((2,))] * 18
    sds = jax.ShapeDtypeStruct
    outs = pl.pallas_call(
        kernel,
        out_shape=(
            sds((PIX, C), BF16),
            sds((7, 7, 2, C), F32),
            sds((2, C), F32),
            sds((2, C), F32),
            sds((2, HID), F32),
            sds((6, 2, C), F32),
            sds((6, 2, C), F32),
        ),
        in_specs=[hbm] * 8,
        out_specs=(hbm,) * 7,
        scratch_shapes=scratch,
        compiler_params=pltpu.CompilerParams(
            collective_id=0, has_side_effects=True, vmem_limit_bytes=64000000
        ),
        name="convnext_step",
    )(
        activations.reshape(PIX, C),
        grad_out.reshape(PIX, C),
        jnp.transpose(kernels, (1, 2, 0, 3)),
        norm_gains,
        norm_shifts,
        w_in,
        b_in,
        w_out,
    )
    grad_in, gk, gg, gs, gb, gwi, gwo = pl.pallas_call(
        hand_over,
        out_shape=tuple(sds(o.shape, o.dtype) for o in outs),
        in_specs=[hbm] * 7,
        out_specs=(hbm,) * 7,
        scratch_shapes=[pltpu.VMEM(o.shape, o.dtype) for o in outs] + [dma((14,))],
        name="hand_over",
    )(*outs)
    return (
        grad_in.reshape(activations.shape),
        jnp.transpose(gk, (2, 0, 1, 3)),
        gg,
        gs,
        gb,
        jnp.transpose(gwi, (1, 2, 0)),
        jnp.transpose(gwo, (1, 2, 0)),
    )


def solution(mesh):
    return jax.shard_map(
        shards,
        mesh=mesh,
        in_specs=(P("rows", "cols", None), P("rows", "cols", None), P(), P(), P(), P(), P(), P()),
        out_specs=(
            P("rows", "cols", None),
            P(),
            P(),
            P(),
            P(),
            P(None, None, ("rows", "cols")),
            P(None, None, ("rows", "cols")),
        ),
        check_vma=False,
    )
```
